512 devices in a mesh: tm: 64 (over y, x, z_lo), freq: 8 (over z_hi, core).
Axes of the slice: x: 4, y: 4, z: 16 (z_hi: 4, z_lo: 4; z = z_hi * 4 + z_lo), core: 2. Of those that a mesh axis runs over, the one named last changes fastest.
Arguments:
- features: bfloat16 [512, 256, 256], P('tm', 'freq'), may hold values from -6 to 6
- upstream: bfloat16 [512, 256, 256], P('tm', 'freq'), may hold values from -6 to 6
- weights: bfloat16 [8, 256, 256], replicated, may hold values from -8 to 8
- gains: float32 [2, 256], replicated, may hold values from 0.5 to 1.5
Outputs:
- grad_input: bfloat16 [512, 256, 256], P('tm', 'freq')
- weight_grads: float32 [8, 256, 256], replicated
- gain_grads: float32 [2, 256], replicated
The draws below stay inside these ranges and needn't reach their ends.
All inputs are finite; a program needn't handle non-finite values.
Results may differ from the reference program's by a relative error of at most 0.02.
Values may be sent and summed in bfloat16 or wider, within the bound.
A program may use at most 128 MiB of HBM per device.

```python
import jax
import jax.numpy as jnp
from jax import lax

D = 256
BINS = 256
HEADS = 4
WINDOW = 128
FRAMES_DEV = 8
FRAMES = 512


def draw_weights(key, part):
    first_key = jax.random.fold_in(jax.random.fold_in(key, 7177), 0)
    matrices = jax.random.normal(first_key, (8, D, D), jnp.float32) * D ** (-0.5)
    return jnp.clip(matrices, -8.0, 8.0).astype(jnp.bfloat16)


def block_scale(stream_key, shape, pieces, low, high):
    factor_of, own = 1.0, jax.random.fold_in(stream_key, 6)
    for position, shards_of in pieces:
        draws = jnp.exp(jax.random.uniform(jax.random.fold_in(own, position), (shards_of,), jnp.float32, low / len(pieces), high / len(pieces)))
        factor_of = factor_of * jnp.repeat(draws, shape[position] // shards_of).reshape([-1 if axis == position else 1 for axis in range(len(shape))])
    return factor_of


def noise(own_key, shape, deviation, reach, pieces=(), kind=jnp.bfloat16):
    values = jax.random.normal(own_key, shape, jnp.float32) * deviation
    if len(pieces) > 0:
        values = block_scale(own_key, shape, pieces, -0.22, 0.18) * values
    return jnp.clip(values, min=-reach, max=reach).astype(kind)


def setup_inputs(seed: int = 0) -> dict:
    arg_keys = jax.random.split(jax.random.key(seed), 5)
    features = noise(arg_keys[0], (FRAMES, BINS, D), 1.0, 6.0, ((0, 64), (1, 8)))
    upstream = noise(arg_keys[1], (FRAMES, BINS, D), 1.0, 6.0, ((0, 64), (1, 8)))
    weights = draw_weights(jax.random.fold_in(arg_keys[4], 71), 0)
    gains = jnp.clip(1.0 + 0.1 * jax.random.normal(arg_keys[3], (2, D), jnp.float32), 0.5, 1.5)
    return dict(features=features, upstream=upstream, weights=weights, gains=gains)


epsilon = 1e-06
masked_score = -1e+30
exact_mode = lax.Precision.HIGHEST

def norm_forward(inputs, gain):
    widened = inputs.astype(jnp.float32)
    inverse = lax.rsqrt(lax.optimization_barrier(jnp.mean(widened * widened, axis=-1, keepdims=True)) + epsilon)
    unit_rows = widened * inverse
    return ((unit_rows * gain).astype(jnp.bfloat16), inverse, unit_rows)

def norm_backward(incoming, inverse, unit_rows, gain):
    scaled = incoming * gain
    result = inverse * (scaled - unit_rows * lax.optimization_barrier(jnp.mean(scaled * unit_rows, axis=-1, keepdims=True)))
    gain_grad = lax.optimization_barrier(jnp.sum((incoming * unit_rows).reshape(-1, unit_rows.shape[-1]), axis=0))
    return (result, gain_grad)

def project(inputs, matrix):
    flat_rows = inputs.reshape(-1, inputs.shape[-1])
    product = jnp.dot(flat_rows, matrix, preferred_element_type=jnp.float32)
    return product.reshape(inputs.shape[:-1] + (matrix.shape[1],))

def project_back(grads, matrices):
    running = jnp.zeros((grads[0].size // grads[0].shape[-1], matrices[0].shape[0]), jnp.float32)
    for grad_part, matrix in zip(grads, matrices):
        flat_rows = grad_part.reshape(-1, grad_part.shape[-1])
        running = running + jnp.dot(flat_rows, matrix.T, preferred_element_type=jnp.float32)
    return running.reshape(grads[0].shape[:-1] + (matrices[0].shape[0],))

def weight_grad(inputs, grads):
    return jnp.dot(inputs.reshape(-1, inputs.shape[-1]).T, grads.reshape(-1, grads.shape[-1]), preferred_element_type=jnp.float32)

def heads_of(array):
    return array.reshape(array.shape[:-1] + (HEADS, array.shape[-1] // HEADS))

def heads_merged(array):
    return array.reshape(array.shape[:-2] + (array.shape[-2] * array.shape[-1],))

def mixing(form, left, right):
    return jnp.einsum(form, left.astype(jnp.float32), right.astype(jnp.float32), precision=exact_mode)

def attend(queries, key_rows, value_rows, allowed, query_form, key_form):
    scaling = queries.shape[-1] ** (-0.5)
    scores = mixing(query_form + ',' + key_form + '->bhqk', queries, key_rows) * scaling
    scores = jnp.where(allowed, scores, masked_score)
    largest = lax.optimization_barrier(jnp.max(scores, axis=-1, keepdims=True))
    log_total = largest + jnp.log(lax.optimization_barrier(jnp.sum(jnp.exp(scores - largest), axis=-1, keepdims=True)))
    attention = jnp.exp(scores - log_total)
    mixed_rows = mixing('bhqk,' + key_form + '->' + query_form, attention.astype(jnp.bfloat16), value_rows).astype(jnp.bfloat16)
    return (mixed_rows, log_total[..., 0], attention)

def query_backward(attention, grad_out, key_rows, value_rows, query_form, key_form):
    scaling = key_rows.shape[-1] ** (-0.5)
    grad_attention = mixing(query_form + ',' + key_form + '->bhqk', grad_out, value_rows)
    row_dot = lax.optimization_barrier(jnp.sum(grad_attention * attention, axis=-1, keepdims=True))
    grad_scores = (attention * (grad_attention - row_dot) * scaling).astype(jnp.bfloat16)
    grad_queries = mixing('bhqk,' + key_form + '->' + query_form, grad_scores, key_rows).astype(jnp.bfloat16)
    return (grad_queries, row_dot[..., 0], grad_scores)

def key_terms(attention, grad_scores, queries, grad_out, query_form, key_form):
    grad_keys = mixing('bhqk,' + query_form + '->' + key_form, grad_scores, queries)
    grad_values = mixing('bhqk,' + query_form + '->' + key_form, attention.astype(jnp.bfloat16), grad_out)
    return (grad_keys, grad_values)

def key_backward(queries, grad_out, log_total, row_dot, key_rows, value_rows, allowed, query_form, key_form):
    scaling = queries.shape[-1] ** (-0.5)
    scores = mixing(query_form + ',' + key_form + '->bhqk', queries, key_rows) * scaling
    scores = jnp.where(allowed, scores, masked_score)
    attention = jnp.exp(scores - log_total[..., None])
    grad_attention = mixing(query_form + ',' + key_form + '->bhqk', grad_out, value_rows)
    grad_scores = (attention * (grad_attention - row_dot[..., None]) * scaling).astype(jnp.bfloat16)
    return key_terms(attention, grad_scores, queries, grad_out, query_form, key_form)

def window_masks(first_frame, frames_dev, window, total_frames):
    half_window = window // 2
    row_ids = jnp.arange(frames_dev, dtype=jnp.int32)[:, None]
    col_ids = jnp.arange(frames_dev + window, dtype=jnp.int32)[None, :]
    frame_ids = first_frame - half_window + col_ids
    inside = (frame_ids >= 0) & (frame_ids < total_frames)
    distance = col_ids - row_ids
    ahead_mask = (distance >= 0) & (distance < window) & inside
    behind_mask = (distance.T >= 1) & (distance.T <= window) & inside.T
    return (ahead_mask, behind_mask)

def reference(features, upstream, weights, gains):
    total_frames = features.shape[0]
    half_window = WINDOW // 2
    block_ids = jnp.arange(total_frames // FRAMES_DEV, dtype=jnp.int32)

    def cut(array, first_frame, count):
        return lax.dynamic_slice_in_dim(array, first_frame, count, 0)

    def padded(array):
        return jnp.pad(array, ((half_window, half_window),) + ((0, 0),) * (array.ndim - 1))
    norm_one, inverse_one, unit_one = norm_forward(features, gains[0])
    query_one = project(norm_one, weights[0]).astype(jnp.bfloat16)
    key_one = project(norm_one, weights[1]).astype(jnp.bfloat16)
    value_one = project(norm_one, weights[2]).astype(jnp.bfloat16)

    def freq_forward(block_index):
        first_frame = (block_index * FRAMES_DEV).astype(jnp.int32)
        mixed_rows, _, _ = attend(heads_of(cut(query_one, first_frame, FRAMES_DEV)), heads_of(cut(key_one, first_frame, FRAMES_DEV)), heads_of(cut(value_one, first_frame, FRAMES_DEV)), True, 'bqhd', 'bkhd')
        return heads_merged(mixed_rows)
    mixed_one = lax.map(freq_forward, block_ids).reshape(features.shape)
    hidden = (features.astype(jnp.float32) + project(mixed_one, weights[3])).astype(jnp.bfloat16)
    norm_two, inverse_two, unit_two = norm_forward(hidden, gains[1])
    query_two = project(norm_two, weights[4]).astype(jnp.bfloat16)
    key_two = project(norm_two, weights[5]).astype(jnp.bfloat16)
    value_two = project(norm_two, weights[6]).astype(jnp.bfloat16)
    pad_key = padded(key_two)
    pad_value = padded(value_two)

    def time_attend(block_index):
        first_frame = (block_index * FRAMES_DEV).astype(jnp.int32)
        ahead_mask, _ = window_masks(first_frame, FRAMES_DEV, WINDOW, total_frames)
        window_keys = heads_of(cut(pad_key, first_frame, FRAMES_DEV + WINDOW))
        window_values = heads_of(cut(pad_value, first_frame, FRAMES_DEV + WINDOW))
        result = attend(heads_of(cut(query_two, first_frame, FRAMES_DEV)), window_keys, window_values, ahead_mask[None, None], 'qbhd', 'kbhd')
        return (result, window_keys, window_values)

    def time_forward(block_index):
        result, _, _ = time_attend(block_index)
        return (heads_merged(result[0]), jnp.transpose(result[1], (2, 0, 1)))
    mixed_two, log_two = lax.map(time_forward, block_ids)
    mixed_two = mixed_two.reshape(features.shape)
    log_two = log_two.reshape(total_frames, features.shape[1], HEADS)
    grad_mixed_two = project_back([upstream], [weights[7]]).astype(jnp.bfloat16)

    def time_query(block_index):
        result, window_keys, window_values = time_attend(block_index)
        first_frame = (block_index * FRAMES_DEV).astype(jnp.int32)
        grad_queries, row_dot, _ = query_backward(result[2], heads_of(cut(grad_mixed_two, first_frame, FRAMES_DEV)), window_keys, window_values, 'qbhd', 'kbhd')
        return (heads_merged(grad_queries), jnp.transpose(row_dot, (2, 0, 1)))
    grad_query_two, row_two = lax.map(time_query, block_ids)
    grad_query_two = grad_query_two.reshape(features.shape)
    row_two = row_two.reshape(total_frames, features.shape[1], HEADS)
    pad_query = padded(query_two)
    pad_grad = padded(grad_mixed_two)
    pad_log = padded(log_two)
    pad_row = padded(row_two)

    def time_key(block_index):
        first_frame = (block_index * FRAMES_DEV).astype(jnp.int32)
        _, behind_mask = window_masks(first_frame, FRAMES_DEV, WINDOW, total_frames)
        grad_keys, grad_values = key_backward(heads_of(cut(pad_query, first_frame, FRAMES_DEV + WINDOW)), heads_of(cut(pad_grad, first_frame, FRAMES_DEV + WINDOW)), jnp.transpose(cut(pad_log, first_frame, FRAMES_DEV + WINDOW), (1, 2, 0)), jnp.transpose(cut(pad_row, first_frame, FRAMES_DEV + WINDOW), (1, 2, 0)), heads_of(cut(key_two, first_frame, FRAMES_DEV)), heads_of(cut(value_two, first_frame, FRAMES_DEV)), behind_mask[None, None], 'qbhd', 'kbhd')
        return (heads_merged(grad_keys.astype(jnp.bfloat16)), heads_merged(grad_values.astype(jnp.bfloat16)))
    grad_key_two, grad_value_two = lax.map(time_key, block_ids)
    grad_key_two = grad_key_two.reshape(features.shape)
    grad_value_two = grad_value_two.reshape(features.shape)
    grad_norm_two = project_back([grad_query_two, grad_key_two, grad_value_two], [weights[4], weights[5], weights[6]])
    hidden_part, gain_two = norm_backward(grad_norm_two, inverse_two, unit_two, gains[1])
    grad_hidden = (upstream.astype(jnp.float32) + hidden_part).astype(jnp.bfloat16)
    grad_mixed_one = project_back([grad_hidden], [weights[3]]).astype(jnp.bfloat16)

    def freq_backward(block_index):
        first_frame = (block_index * FRAMES_DEV).astype(jnp.int32)
        queries = heads_of(cut(query_one, first_frame, FRAMES_DEV))
        key_rows = heads_of(cut(key_one, first_frame, FRAMES_DEV))
        value_rows = heads_of(cut(value_one, first_frame, FRAMES_DEV))
        grad_out = heads_of(cut(grad_mixed_one, first_frame, FRAMES_DEV))
        _, _, attention = attend(queries, key_rows, value_rows, True, 'bqhd', 'bkhd')
        grad_queries, _, grad_scores = query_backward(attention, grad_out, key_rows, value_rows, 'bqhd', 'bkhd')
        grad_keys, grad_values = key_terms(attention, grad_scores, queries, grad_out, 'bqhd', 'bkhd')
        return (heads_merged(grad_queries), heads_merged(grad_keys.astype(jnp.bfloat16)), heads_merged(grad_values.astype(jnp.bfloat16)))
    grad_query_one, grad_key_one, grad_value_one = lax.map(freq_backward, block_ids)
    grad_query_one = grad_query_one.reshape(features.shape)
    grad_key_one = grad_key_one.reshape(features.shape)
    grad_value_one = grad_value_one.reshape(features.shape)
    grad_norm_one = project_back([grad_query_one, grad_key_one, grad_value_one], [weights[0], weights[1], weights[2]])
    input_part, gain_one = norm_backward(grad_norm_one, inverse_one, unit_one, gains[0])
    grad_input = (grad_hidden.astype(jnp.float32) + input_part).astype(jnp.bfloat16)
    inv_root = (features.shape[0] * features.shape[1]) ** (-0.5)
    weight_grads = jnp.stack([weight_grad(norm_one, grad_query_one), weight_grad(norm_one, grad_key_one), weight_grad(norm_one, grad_value_one), weight_grad(mixed_one, grad_hidden), weight_grad(norm_two, grad_query_two), weight_grad(norm_two, grad_key_two), weight_grad(norm_two, grad_value_two), weight_grad(mixed_two, upstream)]) * inv_root
    gain_grads = jnp.stack([gain_one, gain_two]) * inv_root
    return (grad_input, weight_grads, gain_grads)
```

```python
import functools

import jax
import jax.numpy as jnp
from jax import lax
from jax.experimental import pallas as pl
from jax.experimental.pallas import tpu as pltpu
from jax.sharding import PartitionSpec as P

HEADS = 4
HALF = 64
EPS = 1e-06
MASKED = -1e30
BF = jnp.bfloat16
F32 = jnp.float32
MESH = pl.DeviceIdType.MESH
NEAR = 4
VMEM_SPEC = pl.BlockSpec(memory_space=pltpu.VMEM)


def dot(a, b):
    return lax.dot_general(a, b, (((1,), (0,)), ((), ())), preferred_element_type=F32)


def dot_t(a, b):
    return lax.dot_general(a, b, (((1,), (1,)), ((), ())), preferred_element_type=F32)


def t_dot(a, b):
    return lax.dot_general(a, b, (((0,), (0,)), ((), ())), preferred_element_type=F32)


def head_mask(head, rows, width, dtype):
    lane = lax.broadcasted_iota(jnp.int32, (rows, width), 1)
    return (lane // (width // HEADS) == head).astype(dtype)


def unit(rows):
    inverse = lax.rsqrt(jnp.mean(rows * rows, axis=-1, keepdims=True) + EPS)
    return inverse, rows * inverse


def unit_backward(incoming, inverse, unit_rows, gain):
    scaled = incoming * gain
    mean = jnp.mean(scaled * unit_rows, axis=-1, keepdims=True)
    return inverse * (scaled - unit_rows * mean)


def greet(count, peer_of):
    barrier = pltpu.get_barrier_semaphore()

    def tell(k, carry):
        pl.semaphore_signal(barrier, inc=1, device_id=peer_of(k), device_id_type=MESH)
        return carry

    lax.fori_loop(1, count, tell, 0)
    return barrier


def send_all(count, me, device_of, source_of, target, sems):
    send_sem, recv_sem = sems

    def step(k, carry):
        p = lax.rem(me + k, count)
        pltpu.make_async_remote_copy(
            src_ref=source_of(p),
            dst_ref=target.at[me],
            send_sem=send_sem.at[p],
            recv_sem=recv_sem.at[me],
            device_id=device_of(p),
            device_id_type=MESH,
        ).start()
        return carry

    lax.fori_loop(1, count, step, 0)


def wait_all(count, me, device_of, source_of, target, sems):
    send_sem, recv_sem = sems

    def step(k, carry):
        p = lax.rem(me + k, count)
        copy = pltpu.make_async_remote_copy(
            src_ref=source_of(p),
            dst_ref=target.at[p],
            send_sem=send_sem.at[p],
            recv_sem=recv_sem.at[p],
            device_id=device_of(p),
            device_id_type=MESH,
        )
        copy.wait_recv()
        copy.wait_send()
        return carry

    lax.fori_loop(1, count, step, 0)


def dma_pair(count):
    return [pltpu.SemaphoreType.DMA((count,)), pltpu.SemaphoreType.DMA((count,))]


def comm_params(collective_id):
    return pltpu.CompilerParams(collective_id=collective_id, has_side_effects=True)


def freq_exchange_kernel(count, x_ref, out_ref, send_sem, recv_sem):
    me = lax.axis_index("freq")

    def device_of(p):
        return {"freq": p}

    barrier = greet(count, lambda k: device_of(lax.rem(me + k, count)))
    pl.semaphore_wait(barrier, count - 1)
    send_all(count, me, device_of, lambda p: x_ref.at[p], out_ref, (send_sem, recv_sem))
    out_ref[me] = x_ref[me]
    wait_all(count, me, device_of, lambda p: x_ref.at[p], out_ref, (send_sem, recv_sem))


def freq_exchange(x, collective_id):
    count = x.shape[0]
    return pl.pallas_call(
        functools.partial(freq_exchange_kernel, count),
        out_shape=jax.ShapeDtypeStruct(x.shape, x.dtype),
        in_specs=[VMEM_SPEC],
        out_specs=VMEM_SPEC,
        scratch_shapes=dma_pair(count),
        compiler_params=comm_params(collective_id),
        name=f"freq_exchange_{collective_id}",
    )(x)


def to_time_kernel(bins, halo, a_ref, b_ref, a_out, b_out, send_a, recv_a, send_b, recv_b):
    count = 2 * bins
    me = lax.axis_index("tm")
    mine = lax.div(me, bins)
    span = bins + halo

    def device_of(p):
        return {"tm": p}

    barrier = greet(count, lambda k: device_of(lax.rem(me + k, count)))
    pl.semaphore_wait(barrier, count - 1)
    arrays = ((a_ref, a_out, send_a, recv_a), (b_ref, b_out, send_b, recv_b))

    def copy_to(part, half, bin_id):
        src, dst, send, recv = part
        slot = me - halo * half
        return pltpu.make_async_remote_copy(
            src_ref=src.at[bin_id],
            dst_ref=dst.at[slot],
            send_sem=send.at[bin_id + bins * half],
            recv_sem=recv.at[slot],
            device_id=device_of(bin_id + bins * half),
            device_id_type=MESH,
        )

    def each_target(action):
        for half in range(2):
            needed = (me < span) if half == 0 else (me >= halo)

            @pl.when(needed)
            def _():
                def step(k, carry):
                    bin_id = lax.rem(me + k, bins)

                    @pl.when(bin_id + bins * half != me)
                    def _():
                        for part in arrays:
                            action(copy_to(part, half, bin_id))

                    return carry

                lax.fori_loop(0, bins, step, 0)

    each_target(lambda copy: copy.start())
    own_slot = me - halo * mine
    own_bin = me - bins * mine
    for src, dst, _, _ in arrays:
        dst[own_slot] = src[own_bin]

    def arrive(slot, carry):
        @pl.when(slot != own_slot)
        def _():
            for src, dst, send, recv in arrays:
                pltpu.make_async_remote_copy(
                    src_ref=src.at[own_bin],
                    dst_ref=dst.at[slot],
                    send_sem=send.at[me],
                    recv_sem=recv.at[slot],
                    device_id=device_of(slot + halo * mine),
                    device_id_type=MESH,
                ).wait_recv()

        return carry

    lax.fori_loop(0, span, arrive, 0)
    each_target(lambda copy: copy.wait_send())


def to_time(a, b, collective_id):
    bins = a.shape[0]
    halo = bins // 2
    shape = (bins + halo,) + a.shape[1:]
    return pl.pallas_call(
        functools.partial(to_time_kernel, bins, halo),
        out_shape=[jax.ShapeDtypeStruct(shape, a.dtype)] * 2,
        in_specs=[VMEM_SPEC] * 2,
        out_specs=[VMEM_SPEC] * 2,
        scratch_shapes=[
            pltpu.SemaphoreType.DMA((2 * bins,)),
            pltpu.SemaphoreType.DMA((bins + halo,)),
            pltpu.SemaphoreType.DMA((2 * bins,)),
            pltpu.SemaphoreType.DMA((bins + halo,)),
        ],
        compiler_params=comm_params(collective_id),
        name="to_time",
    )(a, b)


def from_time_kernel(bins, x_ref, out_ref, send_sem, recv_sem):
    index = lax.axis_index("tm")
    base = lax.div(index, bins) * bins
    me = index - base

    def device_of(p):
        return {"tm": base + p}

    barrier = greet(bins, lambda k: device_of(lax.rem(me + k, bins)))
    pl.semaphore_wait(barrier, bins - 1)
    send_all(bins, me, device_of, lambda p: x_ref.at[p], out_ref, (send_sem, recv_sem))
    out_ref[me] = x_ref[me]
    wait_all(bins, me, device_of, lambda p: x_ref.at[p], out_ref, (send_sem, recv_sem))


def from_time(x, collective_id):
    bins = x.shape[0]
    return pl.pallas_call(
        functools.partial(from_time_kernel, bins),
        out_shape=jax.ShapeDtypeStruct(x.shape, x.dtype),
        in_specs=[VMEM_SPEC],
        out_specs=VMEM_SPEC,
        scratch_shapes=dma_pair(bins),
        compiler_params=comm_params(collective_id),
        name="from_time",
    )(x)


def reduce_kernel(
    plane, near, far, w_ref, g_ref, out_ref, gain_ref,
    plane_in, near_src, near_in, far_src, far_in, back_src, back_in, last_src, last_in,
    gain_src, gain_plane, gain_near, gain_far, *sems
):
    tm, freq = lax.axis_index("tm"), lax.axis_index("freq")
    core, high = lax.rem(freq, 2), lax.div(freq, 2)
    low = lax.rem(tm, near)
    column = lax.div(tm, near)
    here = column * 2 + core

    def in_plane(p):
        return {"tm": lax.div(p, 2) * near + low, "freq": high * 2 + lax.rem(p, 2)}

    def in_near(p):
        return {"tm": column * near + p, "freq": freq}

    def in_far(p):
        return {"tm": tm, "freq": p * 2 + core}

    pairs = [(sems[2 * i], sems[2 * i + 1]) for i in range(len(sems) // 2)]
    barrier = greet(plane, lambda k: in_plane(lax.rem(here + k, plane)))
    greet(near, lambda k: in_near(lax.rem(low + k, near)))
    greet(far, lambda k: in_far(lax.rem(high + k, far)))
    pl.semaphore_wait(barrier, plane + near + far - 3)

    def both(count, me, device_of, source_of, target, sem, gsrc, gtarget, gsem):
        send_all(count, me, device_of, source_of, target, sem)
        send_all(count, me, device_of, lambda p: gsrc, gtarget, gsem)

    def waited(count, me, device_of, source_of, target, sem, gsrc, gtarget, gsem):
        wait_all(count, me, device_of, source_of, target, sem)
        wait_all(count, me, device_of, lambda p: gsrc, gtarget, gsem)

    def total(ref, count):
        return lax.fori_loop(
            1, count, lambda i, acc: acc + ref[i].astype(F32), ref[0].astype(F32)
        )

    first = (plane, here, in_plane, lambda p: w_ref.at[p], plane_in, pairs[0], g_ref, gain_plane, pairs[1])
    both(*first)
    plane_in[here] = w_ref[here]
    gain_plane[here] = g_ref[...]
    waited(*first)
    rows = near_src.shape[1]
    near_src[...] = total(plane_in, plane).reshape(near, rows, near_src.shape[2])
    gain_src[0] = total(gain_plane, plane)

    second = (near, low, in_near, lambda p: near_src.at[p], near_in, pairs[2], gain_src.at[0], gain_near, pairs[3])
    both(*second)
    near_in[low] = near_src[low]
    gain_near[low] = gain_src[0]
    waited(*second)
    far_src[...] = total(near_in, near)
    gain_src[1] = total(gain_near, near)

    third = (far, high, in_far, lambda p: far_src, far_in, pairs[4], gain_src.at[1], gain_far, pairs[5])
    both(*third)
    far_in[high] = far_src[...]
    gain_far[high] = gain_src[1]
    waited(*third)
    back_src[...] = total(far_in, far)
    gain_ref[...] = total(gain_far, far)

    send_all(near, low, in_near, lambda p: back_src, back_in, pairs[6])
    back_in[low] = back_src[...]
    wait_all(near, low, in_near, lambda p: back_src, back_in, pairs[6])
    last_src[...] = back_in[...].reshape(last_src.shape).astype(last_src.dtype)

    send_all(plane, here, in_plane, lambda p: last_src, last_in, pairs[7])
    last_in[here] = last_src[...]
    wait_all(plane, here, in_plane, lambda p: last_src, last_in, pairs[7])
    out_ref[...] = last_in[...].astype(F32)


def reduce_over_devices(w, g, collective_id):
    plane, rows, width = w.shape
    near, far = NEAR, lax.axis_size("freq") // 2
    part = rows // near
    gain = g.shape
    counts = [plane, plane, near, near, far, far, near, plane]
    return pl.pallas_call(
        functools.partial(reduce_kernel, plane, near, far),
        out_shape=[jax.ShapeDtypeStruct(w.shape, F32), jax.ShapeDtypeStruct(gain, F32)],
        in_specs=[VMEM_SPEC] * 2,
        out_specs=[VMEM_SPEC] * 2,
        scratch_shapes=[
            pltpu.VMEM((plane, rows, width), BF),
            pltpu.VMEM((near, part, width), F32),
            pltpu.VMEM((near, part, width), F32),
            pltpu.VMEM((part, width), F32),
            pltpu.VMEM((far, part, width), F32),
            pltpu.VMEM((part, width), F32),
            pltpu.VMEM((near, part, width), F32),
            pltpu.VMEM((rows, width), BF),
            pltpu.VMEM((plane, rows, width), BF),
            pltpu.VMEM((2,) + gain, F32),
            pltpu.VMEM((plane,) + gain, F32),
            pltpu.VMEM((near,) + gain, F32),
            pltpu.VMEM((far,) + gain, F32),
        ]
        + [sem for count in counts for sem in dma_pair(count)],
        compiler_params=comm_params(collective_id),
        name="reduce_over_devices",
    )(w, g)


def freq_forward_kernel(x_ref, w_ref, gain_ref, h_ref, q_ref, k_ref, v_ref, o_ref, p_ref):
    rows, width = x_ref.shape
    x = x_ref[...].astype(F32)
    _, unit_rows = unit(x)
    norm = (unit_rows * gain_ref[0:1, :]).astype(BF)
    scale = (width // HEADS) ** (-0.5)
    q_ref[...] = dot(norm, w_ref[0]).astype(BF)
    k_ref[...] = dot(norm, w_ref[1]).astype(BF)
    v_ref[...] = dot(norm, w_ref[2]).astype(BF)
    mixed = jnp.zeros((rows, width), F32)
    for head in range(HEADS):
        mask = head_mask(head, rows, width, BF)
        scores = dot_t(q_ref[...] * mask, k_ref[...]) * scale
        e = jnp.exp(scores - jnp.max(scores, axis=-1, keepdims=True))
        p = e * (1.0 / jnp.sum(e, axis=-1, keepdims=True))
        p_ref[head] = p
        mixed = mixed + dot(p.astype(BF), v_ref[...] * mask)
    o_ref[...] = mixed.astype(BF)
    h_ref[...] = (x + dot(o_ref[...], w_ref[3])).astype(BF)


def freq_backward_kernel(
    scale_out, x_ref, gh_ref, q_ref, k_ref, v_ref, o_ref, p_ref, w_ref, gain_ref, gi_ref, wg_ref, gg_ref
):
    rows, width = x_ref.shape
    scale = (width // HEADS) ** (-0.5)
    gain = gain_ref[0:1, :]
    inverse, unit_rows = unit(x_ref[...].astype(F32))
    norm = (unit_rows * gain).astype(BF)
    go = dot_t(gh_ref[...], w_ref[3]).astype(BF)
    gq = jnp.zeros((rows, width), F32)
    gk = jnp.zeros((rows, width), F32)
    gv = jnp.zeros((rows, width), F32)
    for head in range(HEADS):
        mask = head_mask(head, rows, width, BF)
        p = p_ref[head]
        go_head = go * mask
        dp = dot_t(go_head, v_ref[...])
        delta = jnp.sum(dp * p, axis=-1, keepdims=True)
        ds = (p * (dp - delta) * scale).astype(BF)
        gq = gq + dot(ds, k_ref[...] * mask)
        gk = gk + t_dot(ds, q_ref[...] * mask)
        gv = gv + t_dot(p.astype(BF), go_head)
    gq, gk, gv = gq.astype(BF), gk.astype(BF), gv.astype(BF)
    gn = dot_t(gq, w_ref[0]) + dot_t(gk, w_ref[1]) + dot_t(gv, w_ref[2])
    gi_ref[...] = (
        gh_ref[...].astype(F32) + unit_backward(gn, inverse, unit_rows, gain)
    ).astype(BF)
    gg_ref[...] = jnp.sum(gn * unit_rows, axis=0, keepdims=True) * scale_out
    wg_ref[0] = (t_dot(norm, gq) * scale_out).astype(BF)
    wg_ref[1] = (t_dot(norm, gk) * scale_out).astype(BF)
    wg_ref[2] = (t_dot(norm, gv) * scale_out).astype(BF)
    wg_ref[3] = (t_dot(o_ref[...], gh_ref[...]) * scale_out).astype(BF)


def time_kernel(
    scale_out, own, h_ref, up_ref, w_ref, gain_ref, gh_ref, wg_ref, gg_ref,
    n_s, q_s, k_s, v_s, go_s, o_s, gq_s, gk_s, gv_s, u_s
):
    blocks, sub, width = h_ref.shape
    rows = blocks * sub
    scale = (width // HEADS) ** (-0.5)
    gain = gain_ref[1:2, :]
    _, unit_rows = unit(h_ref[...].astype(F32).reshape(rows, width))
    n_s[...] = (unit_rows * gain).astype(BF)
    q_s[...] = dot(n_s[...], w_ref[4]).astype(BF)
    k_s[...] = dot(n_s[...], w_ref[5]).astype(BF)
    v_s[...] = dot(n_s[...], w_ref[6]).astype(BF)
    u_s[...] = up_ref[...].astype(F32).reshape(rows, width).astype(BF)
    go_s[...] = dot_t(u_s[...], w_ref[7]).astype(BF)
    gk_s[...] = jnp.zeros_like(gk_s)
    gv_s[...] = jnp.zeros_like(gv_s)

    queries, keys = 2 * HALF, 4 * HALF
    offset = lax.broadcasted_iota(jnp.int32, (queries, keys), 1) - lax.broadcasted_iota(
        jnp.int32, (queries, keys), 0
    )

    def block(i, carry):
        q_at = pl.ds(pl.multiple_of(i * queries, queries), queries)
        k_at = pl.ds(pl.multiple_of(i * HALF, HALF), keys)
        q, go, k, v = q_s[q_at, :], go_s[q_at, :], k_s[k_at, :], v_s[k_at, :]
        distance = offset - HALF * i
        allowed = (distance >= -HALF) & (distance < HALF)
        mixed = jnp.zeros((queries, width), F32)
        gq = jnp.zeros((queries, width), F32)
        gk = jnp.zeros((keys, width), F32)
        gv = jnp.zeros((keys, width), F32)
        for head in range(HEADS):
            mask = head_mask(head, queries, width, BF)
            key_mask = head_mask(head, keys, width, BF)
            q_head, go_head = q * mask, go * mask
            scores = jnp.where(allowed, dot_t(q_head, k) * scale, MASKED)
            e = jnp.exp(scores - jnp.max(scores, axis=-1, keepdims=True))
            p = e * (1.0 / jnp.sum(e, axis=-1, keepdims=True))
            p_half = p.astype(BF)
            mixed = mixed + dot(p_half, v * key_mask)
            dp = dot_t(go_head, v)
            delta = jnp.sum(dp * p, axis=-1, keepdims=True)
            ds = (p * (dp - delta) * scale).astype(BF)
            gq = gq + dot(ds, k * key_mask)
            gk = gk + t_dot(ds, q_head)
            gv = gv + t_dot(p_half, go_head)
        o_s[q_at, :] = mixed.astype(BF)
        gq_s[q_at, :] = gq.astype(BF)
        gk_s[k_at, :] += gk
        gv_s[k_at, :] += gv
        return carry

    lax.fori_loop(0, rows // queries, block, 0)

    half = lax.div(lax.axis_index("tm"), own // sub)
    first = pl.multiple_of(half * (own // 2), own // 2)
    at = pl.ds(first, own)
    gq, gk, gv = gq_s[at, :], gk_s[at, :].astype(BF), gv_s[at, :].astype(BF)
    gn = dot_t(gq, w_ref[4]) + dot_t(gk, w_ref[5]) + dot_t(gv, w_ref[6])
    own_blocks = pl.ds(lax.div(first, sub), own // sub)
    inverse, unit_own = unit(h_ref[own_blocks].astype(F32).reshape(own, width))
    upstream = u_s[at, :]
    gh = upstream.astype(F32) + unit_backward(gn, inverse, unit_own, gain)
    gh_ref[...] = gh.reshape(own // sub, sub, width).astype(BF)
    gg_ref[...] = jnp.sum(gn * unit_own, axis=0, keepdims=True) * scale_out
    norm = n_s[at, :]
    wg_ref[0] = (t_dot(norm, gq) * scale_out).astype(BF)
    wg_ref[1] = (t_dot(norm, gk) * scale_out).astype(BF)
    wg_ref[2] = (t_dot(norm, gv) * scale_out).astype(BF)
    wg_ref[3] = (t_dot(o_s[at, :], upstream) * scale_out).astype(BF)


def per_device(features, upstream, weights, gains):
    frames, bins, width = features.shape
    rows = bins * lax.axis_size("freq")
    frame_total = frames * lax.axis_size("tm")
    scale_out = (frame_total * rows) ** (-0.5)
    shape = jax.ShapeDtypeStruct

    x = freq_exchange(features, 0).reshape(rows, width)
    hidden, q, k, v, mixed, p = pl.pallas_call(
        freq_forward_kernel,
        out_shape=[shape((rows, width), BF)] * 5 + [shape((HEADS, rows, rows), F32)],
        name="freq_forward",
    )(x, weights, gains)
    back = freq_exchange(hidden.reshape(features.shape), 1)
    h_time, up_time = to_time(back.transpose(1, 0, 2), upstream.transpose(1, 0, 2), 2)
    blocks = h_time.shape[0]
    own = bins * frames
    all_rows = blocks * frames
    half_rows = pltpu.VMEM((all_rows, width), BF)
    full_rows = pltpu.VMEM((all_rows, width), F32)
    gh_time, time_grads, time_gain = pl.pallas_call(
        functools.partial(time_kernel, scale_out, own),
        out_shape=[
            shape((bins, frames, width), BF),
            shape((4, width, width), BF),
            shape((1, width), F32),
        ],
        scratch_shapes=[half_rows] * 7 + [full_rows] * 2 + [half_rows],
        name="time_attention",
    )(h_time, up_time, weights, gains)
    gh_local = from_time(gh_time, 3).transpose(1, 0, 2)
    gh = freq_exchange(gh_local, 4).reshape(rows, width)
    gi, freq_grads, freq_gain = pl.pallas_call(
        functools.partial(freq_backward_kernel, scale_out),
        out_shape=[
            shape((rows, width), BF),
            shape((4, width, width), BF),
            shape((1, width), F32),
        ],
        name="freq_backward",
    )(x, gh, q, k, v, mixed, p, weights, gains)
    grad_input = freq_exchange(gi.reshape(features.shape), 5)
    plane = lax.axis_size("tm") // NEAR * 2
    stacked = jnp.concatenate([freq_grads, time_grads], axis=0)
    gain_rows = jnp.concatenate([freq_gain, time_gain], axis=0).reshape(4, width // 2)
    gain_rows = jnp.pad(gain_rows, ((0, 4), (0, 0)))
    sums, gain_sums = reduce_over_devices(stacked.reshape(plane, -1, width), gain_rows, 6)
    return (
        grad_input,
        sums.reshape(8, width, width),
        gain_sums[:4].reshape(2, width),
    )


def solution(mesh):
    return jax.shard_map(
        per_device,
        mesh=mesh,
        in_specs=(P("tm", "freq", None), P("tm", "freq", None), P(), P()),
        out_specs=(P("tm", "freq", None), P(), P()),
        check_vma=False,
    )
```

```python
import functools

import jax
import jax.numpy as jnp
from jax import lax
from jax.experimental import pallas as pl
from jax.experimental.pallas import tpu as pltpu
from jax.sharding import PartitionSpec as P

HEADS = 4
HALF = 64
EPS = 1e-06
MASKED = -1e30
BF = jnp.bfloat16
F32 = jnp.float32
MESH = pl.DeviceIdType.MESH
NEAR = 4
VMEM_SPEC = pl.BlockSpec(memory_space=pltpu.VMEM)


def dot(a, b):
    return lax.dot_general(a, b, (((1,), (0,)), ((), ())), preferred_element_type=F32)


def dot_t(a, b):
    return lax.dot_general(a, b, (((1,), (1,)), ((), ())), preferred_element_type=F32)


def t_dot(a, b):
    return lax.dot_general(a, b, (((0,), (0,)), ((), ())), preferred_element_type=F32)


def head_mask(head, rows, width, dtype):
    lane = lax.broadcasted_iota(jnp.int32, (rows, width), 1)
    return (lane // (width // HEADS) == head).astype(dtype)


def unit(rows):
    inverse = lax.rsqrt(jnp.mean(rows * rows, axis=-1, keepdims=True) + EPS)
    return inverse, rows * inverse


def unit_backward(incoming, inverse, unit_rows, gain):
    scaled = incoming * gain
    mean = jnp.mean(scaled * unit_rows, axis=-1, keepdims=True)
    return inverse * (scaled - unit_rows * mean)


class Exchange:
    def __init__(self, count, me, device_of, source_of, target, sems):
        self.count, self.me, self.device_of = count, me, device_of
        self.source_of, self.target, self.sems = source_of, target, sems

    def copy(self, p, slot):
        send_sem, recv_sem = self.sems
        return pltpu.make_async_remote_copy(
            src_ref=self.source_of(p),
            dst_ref=self.target.at[slot],
            send_sem=send_sem.at[p],
            recv_sem=recv_sem.at[slot],
            device_id=self.device_of(p),
            device_id_type=MESH,
        )

    def others(self, action):
        def step(k, carry):
            action(lax.rem(self.me + k, self.count))
            return carry

        lax.fori_loop(1, self.count, step, 0)

    def start(self):
        self.others(lambda p: self.copy(p, self.me).start())
        self.target[self.me] = self.source_of(self.me)[...]

    def wait(self):
        def step(p):
            copy = self.copy(p, p)
            copy.wait_recv()
            copy.wait_send()

        self.others(step)


class ToTime:
    def __init__(self, bins, me, source, target, sems):
        self.bins, self.halo, self.me = bins, bins // 2, me
        self.mine = lax.div(me, bins)
        self.source, self.target, self.sems = source, target, sems

    def copy(self, bin_id, half, slot):
        send_sem, recv_sem = self.sems
        return pltpu.make_async_remote_copy(
            src_ref=self.source.at[bin_id],
            dst_ref=self.target.at[slot],
            send_sem=send_sem.at[bin_id + self.bins * half],
            recv_sem=recv_sem.at[slot],
            device_id={"tm": bin_id + self.bins * half},
            device_id_type=MESH,
        )

    def each_target(self, action):
        for half in range(2):
            needed = (self.me < self.bins + self.halo) if half == 0 else (self.me >= self.halo)

            @pl.when(needed)
            def _():
                def step(k, carry):
                    bin_id = lax.rem(self.me + k, self.bins)

                    @pl.when(bin_id + self.bins * half != self.me)
                    def _():
                        action(self.copy(bin_id, half, self.me - self.halo * half))

                    return carry

                lax.fori_loop(0, self.bins, step, 0)

    def start(self):
        self.each_target(lambda copy: copy.start())
        own = self.me - self.halo * self.mine
        self.target[own] = self.source[self.me - self.bins * self.mine]

    def wait(self):
        own = self.me - self.halo * self.mine
        send_sem, recv_sem = self.sems

        def arrive(slot, carry):
            @pl.when(slot != own)
            def _():
                pltpu.make_async_remote_copy(
                    src_ref=self.source.at[0],
                    dst_ref=self.target.at[slot],
                    send_sem=send_sem.at[0],
                    recv_sem=recv_sem.at[slot],
                    device_id={"tm": slot + self.halo * self.mine},
                    device_id_type=MESH,
                ).wait_recv()

            return carry

        lax.fori_loop(0, self.bins + self.halo, arrive, 0)
        self.each_target(lambda copy: copy.wait_send())


def total(ref, count):
    return lax.fori_loop(1, count, lambda i, acc: acc + ref[i].astype(F32), ref[0].astype(F32))


def swapped(value):
    return jnp.swapaxes(value.astype(F32), 0, 1).astype(BF)


def layer_kernel(scale_out, names, x_ref, up_ref, w_ref, gain_ref, gi_ref, sum_ref, gain_out, *scratch):
    s = dict(zip(names, scratch))
    frames, bins, width = x_ref.shape
    scale = (width // HEADS) ** (-0.5)
    tm, freq = lax.axis_index("tm"), lax.axis_index("freq")
    tm_count, freq_count = s["rs_time_in"].shape[0] // 2 * NEAR, frames
    core, high = lax.rem(freq, 2), lax.div(freq, 2)
    low, column = lax.rem(tm, NEAR), lax.div(tm, NEAR)
    here = column * 2 + core
    plane, far = s["rs_time_in"].shape[0], freq_count // 2
    rows = bins * freq_count
    base = lax.div(tm, bins) * bins

    def in_freq(p):
        return {"freq": p}

    def in_tm(p):
        return {"tm": p}

    def in_half(p):
        return {"tm": base + p}

    def in_plane(p):
        return {"tm": lax.div(p, 2) * NEAR + low, "freq": high * 2 + lax.rem(p, 2)}

    def in_near(p):
        return {"tm": column * NEAR + p, "freq": freq}

    def in_far(p):
        return {"tm": tm, "freq": p * 2 + core}

    def sems(name):
        return s[name + "_send"], s[name + "_recv"]

    barrier = pltpu.get_barrier_semaphore()

    def tell(first, last, peer_of):
        def step(k, carry):
            pl.semaphore_signal(barrier, inc=1, device_id=peer_of(k), device_id_type=MESH)
            return carry

        lax.fori_loop(first, last, step, 0)

    tell(1, freq_count, lambda k: in_freq(lax.rem(freq + k, freq_count)))
    tell(0, plane // 2, lambda k: in_plane(lax.rem(column + k, plane // 2) * 2 + 1 - core))
    tell(1, tm_count, lambda k: in_tm(lax.rem(tm + k, tm_count)))
    s["up_t"][...] = swapped(up_ref[...])
    pl.semaphore_wait(barrier, freq_count - 1 + plane // 2 + tm_count - 1)

    to_frames = Exchange(freq_count, freq, in_freq, lambda p: x_ref.at[p], s["x_f"], sems("x"))
    to_frames.start()
    up_time = ToTime(bins, tm, s["up_t"], s["up_w"], sems("up"))
    up_time.start()
    to_frames.wait()

    gain = gain_ref[0:1, :]
    x = s["x_f"][...].astype(F32).reshape(rows, width)
    _, unit_rows = unit(x)
    norm = (unit_rows * gain).astype(BF)
    s["n1"][...] = norm
    s["q1"][...] = dot(norm, w_ref[0]).astype(BF)
    s["k1"][...] = dot(norm, w_ref[1]).astype(BF)
    s["v1"][...] = dot(norm, w_ref[2]).astype(BF)
    mixed = jnp.zeros((rows, width), F32)
    for head in range(HEADS):
        mask = head_mask(head, rows, width, BF)
        scores = dot_t(s["q1"][...] * mask, s["k1"][...]) * scale
        e = jnp.exp(scores - jnp.max(scores, axis=-1, keepdims=True))
        p = e * (1.0 / jnp.sum(e, axis=-1, keepdims=True))
        s["p1"][head] = p
        mixed = mixed + dot(p.astype(BF), s["v1"][...] * mask)
    s["o1"][...] = mixed.astype(BF)
    hidden = x + dot(s["o1"][...], w_ref[3])
    s["h_f"][...] = hidden.reshape(x_ref.shape).astype(BF)
    h_back = Exchange(freq_count, freq, in_freq, lambda p: s["h_f"].at[p], s["h_l"], sems("h"))
    h_back.start()

    up_time.wait()
    blocks, sub = s["up_w"].shape[:2]
    all_rows, own = blocks * sub, bins * sub
    s["up"][...] = s["up_w"][...].astype(F32).reshape(all_rows, width).astype(BF)
    s["go2"][...] = dot_t(s["up"][...], w_ref[7]).astype(BF)
    s["gk2"][...] = jnp.zeros_like(s["gk2"])
    s["gv2"][...] = jnp.zeros_like(s["gv2"])
    h_back.wait()
    s["h_t"][...] = swapped(s["h_l"][...])
    h_time = ToTime(bins, tm, s["h_t"], s["h_w"], sems("hw"))
    h_time.start()
    h_time.wait()

    gain = gain_ref[1:2, :]
    _, unit_rows = unit(s["h_w"][...].astype(F32).reshape(all_rows, width))
    norm = (unit_rows * gain).astype(BF)
    s["n2"][...] = norm
    s["q2"][...] = dot(norm, w_ref[4]).astype(BF)
    s["k2"][...] = dot(norm, w_ref[5]).astype(BF)
    s["v2"][...] = dot(norm, w_ref[6]).astype(BF)
    queries, keys = 2 * HALF, 4 * HALF
    offset = lax.broadcasted_iota(jnp.int32, (queries, keys), 1) - lax.broadcasted_iota(
        jnp.int32, (queries, keys), 0
    )

    def block(i, carry):
        q_at = pl.ds(pl.multiple_of(i * queries, queries), queries)
        k_at = pl.ds(pl.multiple_of(i * HALF, HALF), keys)
        q, go, k, v = s["q2"][q_at, :], s["go2"][q_at, :], s["k2"][k_at, :], s["v2"][k_at, :]
        distance = offset - HALF * i
        allowed = (distance >= -HALF) & (distance < HALF)
        mixed = jnp.zeros((queries, width), F32)
        gq = jnp.zeros((queries, width), F32)
        gk = jnp.zeros((keys, width), F32)
        gv = jnp.zeros((keys, width), F32)
        for head in range(HEADS):
            mask = head_mask(head, queries, width, BF)
            key_mask = head_mask(head, keys, width, BF)
            q_head, go_head = q * mask, go * mask
            scores = jnp.where(allowed, dot_t(q_head, k) * scale, MASKED)
            e = jnp.exp(scores - jnp.max(scores, axis=-1, keepdims=True))
            p = e * (1.0 / jnp.sum(e, axis=-1, keepdims=True))
            p_half = p.astype(BF)
            mixed = mixed + dot(p_half, v * key_mask)
            dp = dot_t(go_head, v)
            delta = jnp.sum(dp * p, axis=-1, keepdims=True)
            ds = (p * (dp - delta) * scale).astype(BF)
            gq = gq + dot(ds, k * key_mask)
            gk = gk + t_dot(ds, q_head)
            gv = gv + t_dot(p_half, go_head)
        s["o2"][q_at, :] = mixed.astype(BF)
        s["gq2"][q_at, :] = gq.astype(BF)
        s["gk2"][k_at, :] += gk
        s["gv2"][k_at, :] += gv
        return carry

    lax.fori_loop(0, all_rows // queries, block, 0)

    half = lax.div(tm, bins)
    first = pl.multiple_of(half * (own // 2), own // 2)
    at = pl.ds(first, own)
    gq, gk, gv = s["gq2"][at, :], s["gk2"][at, :].astype(BF), s["gv2"][at, :].astype(BF)
    gn = dot_t(gq, w_ref[4]) + dot_t(gk, w_ref[5]) + dot_t(gv, w_ref[6])
    own_blocks = pl.ds(half * (bins // 2), bins)
    inverse, unit_own = unit(s["h_w"][own_blocks].astype(F32).reshape(own, width))
    upstream = s["up"][at, :]
    gh = upstream.astype(F32) + unit_backward(gn, inverse, unit_own, gain)
    s["gh_t"][...] = gh.reshape(bins, sub, width).astype(BF)
    gh_back = Exchange(bins, tm - base, in_half, lambda p: s["gh_t"].at[p], s["gh_b"], sems("ghb"))
    gh_back.start()

    def place(name, index, value):
        per = width // s[name].shape[1]
        s[name][pl.ds(index * per, per)] = (
            (value * scale_out).reshape(per, s[name].shape[1], width).astype(BF)
        )

    def reduction(name):
        def stage(short, count, me, device_of, source_of, target):
            full = name + "_" + short
            return Exchange(count, me, device_of, source_of, s[target], sems(full))

        stack, result = s["wg_" + name], sum_ref.at[0 if name == "freq" else 1]
        return [
            stage("rs", plane, here, in_plane, lambda p: stack.at[p], "rs_" + name + "_in"),
            stage("near", NEAR, low, in_near, lambda p: s["near_" + name].at[p], "near_" + name + "_in"),
            stage("far", far, high, in_far, lambda p: s["far_" + name], "far_" + name + "_in"),
            stage("back", NEAR, low, in_near, lambda p: s["back_" + name], "back_" + name + "_in"),
            Exchange(plane, here, in_plane, lambda p: s["last_" + name], result, sems(name + "_last")),
        ]

    def after_plane(name):
        near = s["near_" + name]
        near[...] = total(s["rs_" + name + "_in"], plane).reshape(near.shape)

    def after_near(name):
        s["far_" + name][...] = total(s["near_" + name + "_in"], NEAR)

    def after_far(name):
        s["back_" + name][...] = total(s["far_" + name + "_in"], far)

    def after_back(name):
        last = s["last_" + name]
        last[...] = s["back_" + name + "_in"][...].reshape(last.shape).astype(BF)

    norm = s["n2"][at, :]
    place("wg_time", 0, t_dot(norm, gq))
    place("wg_time", 1, t_dot(norm, gk))
    place("wg_time", 2, t_dot(norm, gv))
    place("wg_time", 3, t_dot(s["o2"][at, :], upstream))
    time_gain = jnp.sum(gn * unit_own, axis=0, keepdims=True) * scale_out
    t_rs, t_near, t_far, t_back, t_last = reduction("time")
    t_rs.start()
    gh_back.wait()
    s["gh_l"][...] = swapped(s["gh_b"][...])
    gh_frames = Exchange(freq_count, freq, in_freq, lambda p: s["gh_l"].at[p], s["gh_f"], sems("gh"))
    gh_frames.start()
    t_rs.wait()
    after_plane("time")
    t_near.start()
    gh_frames.wait()

    gain = gain_ref[0:1, :]
    inverse, unit_rows = unit(s["x_f"][...].astype(F32).reshape(rows, width))
    gh32 = s["gh_f"][...].astype(F32).reshape(rows, width)
    gh = gh32.astype(BF)
    go = dot_t(gh, w_ref[3]).astype(BF)
    gq = jnp.zeros((rows, width), F32)
    gk = jnp.zeros((rows, width), F32)
    gv = jnp.zeros((rows, width), F32)
    for head in range(HEADS):
        mask = head_mask(head, rows, width, BF)
        p = s["p1"][head]
        go_head = go * mask
        dp = dot_t(go_head, s["v1"][...])
        delta = jnp.sum(dp * p, axis=-1, keepdims=True)
        ds = (p * (dp - delta) * scale).astype(BF)
        gq = gq + dot(ds, s["k1"][...] * mask)
        gk = gk + t_dot(ds, s["q1"][...] * mask)
        gv = gv + t_dot(p.astype(BF), go_head)
    gq, gk, gv = gq.astype(BF), gk.astype(BF), gv.astype(BF)
    gn = dot_t(gq, w_ref[0]) + dot_t(gk, w_ref[1]) + dot_t(gv, w_ref[2])
    gi = gh32 + unit_backward(gn, inverse, unit_rows, gain)
    s["gi_f"][...] = gi.reshape(x_ref.shape).astype(BF)
    gi_back = Exchange(freq_count, freq, in_freq, lambda p: s["gi_f"].at[p], gi_ref, sems("gi"))
    gi_back.start()
    norm = s["n1"][...]
    place("wg_freq", 0, t_dot(norm, gq))
    place("wg_freq", 1, t_dot(norm, gk))
    place("wg_freq", 2, t_dot(norm, gv))
    place("wg_freq", 3, t_dot(s["o1"][...], gh))
    f_rs, f_near, f_far, f_back, f_last = reduction("freq")
    f_rs.start()

    freq_gain = jnp.sum(gn * unit_rows, axis=0, keepdims=True) * scale_out
    s["g_0"][...] = jnp.concatenate([freq_gain, time_gain], axis=0)

    def gain_stage(number, count, me, device_of):
        source = s[f"g_{number}"]
        return Exchange(count, me, device_of, lambda p: source, s[f"g_in_{number}"], sems(f"g{number}"))

    g_plane = gain_stage(0, plane, here, in_plane)
    g_near = gain_stage(1, NEAR, low, in_near)
    g_far = gain_stage(2, far, high, in_far)
    g_plane.start()

    t_near.wait()
    after_near("time")
    t_far.start()
    f_rs.wait()
    after_plane("freq")
    f_near.start()
    g_plane.wait()
    s["g_1"][...] = total(s["g_in_0"], plane)
    g_near.start()
    t_far.wait()
    after_far("time")
    t_back.start()
    f_near.wait()
    after_near("freq")
    f_far.start()
    g_near.wait()
    s["g_2"][...] = total(s["g_in_1"], NEAR)
    g_far.start()
    t_back.wait()
    after_back("time")
    t_last.start()
    f_far.wait()
    after_far("freq")
    f_back.start()
    g_far.wait()
    gain_out[...] = total(s["g_in_2"], far)
    f_back.wait()
    after_back("freq")
    f_last.start()
    gi_back.wait()
    t_last.wait()
    f_last.wait()


def per_device(features, upstream, weights, gains):
    frames, bins, width = features.shape
    freq_count, tm_count = lax.axis_size("freq"), lax.axis_size("tm")
    rows = bins * freq_count
    scale_out = (frames * tm_count * rows) ** (-0.5)
    shape = jax.ShapeDtypeStruct
    plane, far = tm_count // NEAR * 2, freq_count // 2
    chunk = 4 * width // plane
    piece = chunk // NEAR
    span = bins + bins // 2
    all_rows = span * frames

    local = ((frames, bins, width), BF)
    turned = ((bins, frames, width), BF)
    window = ((span, frames, width), BF)
    flat = ((rows, width), BF)
    tall = ((all_rows, width), BF)
    buffers = dict(
        up_t=turned, up_w=window, x_f=local, n1=flat, q1=flat, k1=flat, v1=flat, o1=flat,
        p1=((HEADS, rows, rows), F32), h_f=local, h_l=local, h_t=turned, h_w=window,
        up=tall, go2=tall, n2=tall, q2=tall, k2=tall, v2=tall, o2=tall, gq2=tall,
        gk2=((all_rows, width), F32), gv2=((all_rows, width), F32),
        gh_t=turned, gh_b=turned, gh_l=local, gh_f=local, gi_f=local,
    )
    counts = dict(x=freq_count, h=freq_count, ghb=bins, gh=freq_count, gi=freq_count)
    for name in ("freq", "time"):
        buffers["wg_" + name] = ((plane, chunk, width), BF)
        buffers["rs_" + name + "_in"] = ((plane, chunk, width), BF)
        buffers["near_" + name] = ((NEAR, piece, width), F32)
        buffers["near_" + name + "_in"] = ((NEAR, piece, width), F32)
        buffers["far_" + name] = ((piece, width), F32)
        buffers["far_" + name + "_in"] = ((far, piece, width), F32)
        buffers["back_" + name] = ((piece, width), F32)
        buffers["back_" + name + "_in"] = ((NEAR, piece, width), F32)
        buffers["last_" + name] = ((chunk, width), BF)
        for stage, count in zip(("rs", "near", "far", "back", "last"), (plane, NEAR, far, NEAR, plane)):
            counts[name + "_" + stage] = count
    for number, count in enumerate((plane, NEAR, far)):
        buffers[f"g_{number}"] = ((2, width), F32)
        buffers[f"g_in_{number}"] = ((count, 2, width), F32)
        counts[f"g{number}"] = count
    names = list(buffers)
    scratch = [pltpu.VMEM(*buffers[name]) for name in names]
    for name, count in counts.items():
        for end in ("_send", "_recv"):
            names.append(name + end)
            scratch.append(pltpu.SemaphoreType.DMA((count,)))
    for name in ("up", "hw"):
        for end, count in (("_send", tm_count), ("_recv", span)):
            names.append(name + end)
            scratch.append(pltpu.SemaphoreType.DMA((count,)))

    grad_input, sums, gain_sums = pl.pallas_call(
        functools.partial(layer_kernel, scale_out, names),
        out_shape=[
            shape(features.shape, BF),
            shape((2, plane, chunk, width), BF),
            shape((2, width), F32),
        ],
        in_specs=[VMEM_SPEC] * 4,
        out_specs=[VMEM_SPEC] * 3,
        scratch_shapes=scratch,
        compiler_params=pltpu.CompilerParams(collective_id=0, has_side_effects=True),
        name="layer",
    )(features, upstream, weights, gains)
    return grad_input, sums.reshape(8, width, width).astype(F32), gain_sums


def solution(mesh):
    return jax.shard_map(
        per_device,
        mesh=mesh,
        in_specs=(P("tm", "freq", None), P("tm", "freq", None), P(), P()),
        out_specs=(P("tm", "freq", None), P(), P()),
        check_vma=False,
    )
```

```python
import functools

import jax
import jax.numpy as jnp
from jax import lax
from jax.experimental import pallas as pl
from jax.experimental.pallas import tpu as pltpu
from jax.sharding import PartitionSpec as P

HEADS = 4
HALF = 64
EPS = 1e-06
MASKED = -1e30
BF = jnp.bfloat16
F32 = jnp.float32
MESH = pl.DeviceIdType.MESH
NEAR = 4
VMEM_SPEC = pl.BlockSpec(memory_space=pltpu.VMEM)


def dot(a, b):
    return lax.dot_general(a, b, (((1,), (0,)), ((), ())), preferred_element_type=F32)


def dot_t(a, b):
    return lax.dot_general(a, b, (((1,), (1,)), ((), ())), preferred_element_type=F32)


def t_dot(a, b):
    return lax.dot_general(a, b, (((0,), (0,)), ((), ())), preferred_element_type=F32)


def unit(rows):
    inverse = lax.rsqrt(jnp.mean(rows * rows, axis=-1, keepdims=True) + EPS)
    return inverse, rows * inverse


def unit_backward(incoming, inverse, unit_rows, gain):
    scaled = incoming * gain
    mean = jnp.mean(scaled * unit_rows, axis=-1, keepdims=True)
    return inverse * (scaled - unit_rows * mean)


class Exchange:
    def __init__(self, count, me, device_of, source_of, target_of, arrivals, sems):
        self.count, self.me, self.device_of = count, me, device_of
        self.source_of, self.target_of, self.arrivals, self.sems = source_of, target_of, arrivals, sems

    def start(self):
        send_sem, recv_sem = self.sems

        def step(k, carry):
            p = lax.rem(self.me + k, self.count)
            pltpu.make_async_remote_copy(
                src_ref=self.source_of(p),
                dst_ref=self.target_of(self.me),
                send_sem=send_sem,
                recv_sem=recv_sem,
                device_id=self.device_of(p),
                device_id_type=MESH,
            ).start()
            return carry

        lax.fori_loop(1, self.count, step, 0)
        self.target_of(self.me)[...] = self.source_of(self.me)[...]

    def wait(self):
        send_sem, recv_sem = self.sems
        copy = pltpu.make_async_remote_copy(
            src_ref=self.arrivals,
            dst_ref=self.arrivals,
            send_sem=send_sem,
            recv_sem=recv_sem,
            device_id=self.device_of(lax.rem(self.me + 1, self.count)),
            device_id_type=MESH,
        )
        copy.wait_recv()
        copy.wait_send()


class ToTime:
    def __init__(self, bins, me, source, target, sems):
        self.bins, self.halo, self.me = bins, bins // 2, me
        self.mine = lax.div(me, bins)
        self.source, self.target, self.sems = source, target, sems

    def copy(self, source, target, half, device):
        return pltpu.make_async_remote_copy(
            src_ref=source,
            dst_ref=target,
            send_sem=self.sems[half],
            recv_sem=self.sems[2],
            device_id={"tm": device},
            device_id_type=MESH,
        )

    def each_half(self, action):
        for half in range(2):
            needed = (self.me < self.bins + self.halo) if half == 0 else (self.me >= self.halo)
            pl.when(needed)(functools.partial(action, half))

    def start(self):
        def send(half):
            def step(k, carry):
                bin_id = lax.rem(self.me + k, self.bins)
                device = bin_id + self.bins * half

                @pl.when(device != self.me)
                def _():
                    slot = self.target.at[self.me - self.halo * half]
                    self.copy(self.source.at[bin_id], slot, half, device).start()

                return carry

            lax.fori_loop(0, self.bins, step, 0)

        self.each_half(send)
        own = self.me - self.halo * self.mine
        self.target[own] = self.source[self.me - self.bins * self.mine]

    def wait(self):
        other = lax.rem(self.me + 1, 2 * self.bins)
        arrivals = self.target.at[pl.ds(0, self.bins + self.halo - 1)]
        self.copy(arrivals, arrivals, 0, other).wait_recv()

        def sent(half):
            @pl.when(self.mine == half)
            def _():
                left = self.source.at[pl.ds(0, self.bins - 1)]
                self.copy(left, left, half, other).wait_send()

            @pl.when(self.mine != half)
            def _():
                self.copy(self.source, self.source, half, other).wait_send()

        self.each_half(sent)


def total(ref, count):
    return lax.fori_loop(1, count, lambda i, acc: acc + ref[i].astype(F32), ref[0].astype(F32))


def swapped(value):
    return jnp.swapaxes(value.astype(F32), 0, 1).astype(BF)


def head_masks(rows, width):
    lane = lax.broadcasted_iota(jnp.int32, (rows, width), 1) // (width // HEADS)
    return [(lane == head).astype(BF) for head in range(HEADS)]


def weights_of(scores):
    e = jnp.exp(scores - jnp.max(scores, axis=0, keepdims=True))
    return e * (1.0 / jnp.sum(e, axis=0, keepdims=True))


def scores_backward(p, dp):
    return (p * (dp - jnp.sum(dp * p, axis=0, keepdims=True))).astype(BF)


def layer_kernel(
    scale_out, names, x_ref, up_ref, gain_ref, w_hbm, gi_ref, sum_ref, gain_out, w_ref, dma, w_sem, *scratch
):
    s = dict(zip(names, scratch))
    frames, bins, width = x_ref.shape
    scale = (width // HEADS) ** (-0.5)
    tm, freq = lax.axis_index("tm"), lax.axis_index("freq")
    plane = s["rs_time"].shape[0]
    tm_count, freq_count = plane // 2 * NEAR, frames
    core, high = lax.rem(freq, 2), lax.div(freq, 2)
    low, column = lax.rem(tm, NEAR), lax.div(tm, NEAR)
    here = column * 2 + core
    far = freq_count // 2
    rows = bins * freq_count
    base = lax.div(tm, bins) * bins

    def in_freq(p):
        return {"freq": p}

    def in_tm(p):
        return {"tm": p}

    def in_half(p):
        return {"tm": base + p}

    def in_plane(p):
        return {"tm": lax.div(p, 2) * NEAR + low, "freq": high * 2 + lax.rem(p, 2)}

    def in_near(p):
        return {"tm": column * NEAR + p, "freq": freq}

    def in_far(p):
        return {"tm": tm, "freq": p * 2 + core}

    used = [0]

    def sems(count=2):
        first = used[0]
        used[0] += count
        return [dma.at[first + i] for i in range(count)]

    def along(group, source_of, target):
        count, me, device_of = group
        arrivals = target.at[pl.ds(0, count - 1)]
        return Exchange(count, me, device_of, source_of, lambda p: target.at[p], arrivals, sems())

    freq_group = (freq_count, freq, in_freq)
    plane_group = (plane, here, in_plane)
    near_group = (NEAR, low, in_near)
    far_group = (far, high, in_far)

    barrier = pltpu.get_barrier_semaphore()

    def tell(first, last, peer_of):
        def step(k, carry):
            pl.semaphore_signal(barrier, inc=1, device_id=peer_of(k), device_id_type=MESH)
            return carry

        lax.fori_loop(first, last, step, 0)

    tell(1, freq_count, lambda k: in_freq(lax.rem(freq + k, freq_count)))
    tell(0, plane // 2, lambda k: in_plane(lax.rem(column + k, plane // 2) * 2 + 1 - core))
    tell(1, tm_count, lambda k: in_tm(lax.rem(tm + k, tm_count)))
    load = pltpu.make_async_copy(w_hbm, w_ref, w_sem)
    load.start()
    s["up_t"][...] = swapped(up_ref[...])
    pl.semaphore_wait(barrier, freq_count - 1 + plane // 2 + tm_count - 1)

    to_frames = along(freq_group, lambda p: x_ref.at[p], s["x_f"])
    to_frames.start()
    up_time = ToTime(bins, tm, s["up_t"], s["up_w"], sems(3))
    up_time.start()
    load.wait()
    to_frames.wait()

    masks = head_masks(rows, width)
    gain = gain_ref[0:1, :]
    x = s["x_f"][...].astype(F32).reshape(rows, width)
    _, unit_rows = unit(x)
    norm = (unit_rows * gain).astype(BF)
    s["n1"][...] = norm
    s["q1"][...] = (dot(norm, w_ref[0]).astype(BF) * scale).astype(BF)
    s["k1"][...] = dot(norm, w_ref[1]).astype(BF)
    s["v1"][...] = dot(norm, w_ref[2]).astype(BF)
    mixed = jnp.zeros((rows, width), F32)
    for head in range(HEADS):
        p = weights_of(dot_t(s["k1"][...], s["q1"][...] * masks[head]))
        s["p1"][head] = p
        mixed = mixed + t_dot(p.astype(BF), s["v1"][...] * masks[head])
    s["o1"][...] = mixed.astype(BF)
    hidden = x + dot(s["o1"][...], w_ref[3])
    s["h_f"][...] = hidden.reshape(x_ref.shape).astype(BF)
    h_back = along(freq_group, lambda p: s["h_f"].at[p], s["h_l"])
    h_back.start()

    up_time.wait()
    blocks, sub = s["up_w"].shape[:2]
    all_rows, own = blocks * sub, bins * sub
    s["up"][...] = s["up_w"][...].astype(F32).reshape(all_rows, width).astype(BF)
    s["go2"][...] = dot_t(s["up"][...], w_ref[7]).astype(BF)
    s["gk2"][...] = jnp.zeros_like(s["gk2"])
    s["gv2"][...] = jnp.zeros_like(s["gv2"])
    h_back.wait()
    s["h_t"][...] = swapped(s["h_l"][...])
    h_time = ToTime(bins, tm, s["h_t"], s["h_w"], sems(3))
    h_time.start()
    h_time.wait()

    gain = gain_ref[1:2, :]
    _, unit_rows = unit(s["h_w"][...].astype(F32).reshape(all_rows, width))
    norm = (unit_rows * gain).astype(BF)
    s["n2"][...] = norm
    s["q2"][...] = (dot(norm, w_ref[4]).astype(BF) * scale).astype(BF)
    s["k2"][...] = dot(norm, w_ref[5]).astype(BF)
    s["v2"][...] = dot(norm, w_ref[6]).astype(BF)
    queries, keys = 2 * HALF, 4 * HALF
    offset = lax.broadcasted_iota(jnp.int32, (keys, queries), 0) - lax.broadcasted_iota(
        jnp.int32, (keys, queries), 1
    )

    def block(i, carry):
        q_at = pl.ds(pl.multiple_of(i * queries, queries), queries)
        k_at = pl.ds(pl.multiple_of(i * HALF, HALF), keys)
        q, go, k, v = s["q2"][q_at, :], s["go2"][q_at, :], s["k2"][k_at, :], s["v2"][k_at, :]
        distance = offset - HALF * i
        allowed = (distance >= -HALF) & (distance < HALF)
        key_masks, query_masks = head_masks(keys, width), head_masks(queries, width)
        mixed = jnp.zeros((queries, width), F32)
        gq = jnp.zeros((queries, width), F32)
        gk = jnp.zeros((keys, width), F32)
        gv = jnp.zeros((keys, width), F32)
        for head in range(HEADS):
            q_head, go_head = q * query_masks[head], go * query_masks[head]
            p = weights_of(jnp.where(allowed, dot_t(k, q_head), MASKED))
            p_half = p.astype(BF)
            ds = scores_backward(p, dot_t(v, go_head))
            mixed = mixed + t_dot(p_half, v * key_masks[head])
            gq = gq + t_dot(ds, k * key_masks[head])
            gk = gk + dot(ds, q_head)
            gv = gv + dot(p_half, go_head)
        s["o2"][q_at, :] = mixed.astype(BF)
        s["gq2"][q_at, :] = (gq * scale).astype(BF)
        s["gk2"][k_at, :] += gk
        s["gv2"][k_at, :] += gv
        return carry

    lax.fori_loop(0, all_rows // queries, block, 0)

    half = lax.div(tm, bins)
    first = pl.multiple_of(half * (own // 2), own // 2)
    at = pl.ds(first, own)
    gq, gk, gv = s["gq2"][at, :], s["gk2"][at, :].astype(BF), s["gv2"][at, :].astype(BF)
    gn = dot_t(gq, w_ref[4]) + dot_t(gk, w_ref[5]) + dot_t(gv, w_ref[6])
    own_blocks = pl.ds(half * (bins // 2), bins)
    inverse, unit_own = unit(s["h_w"][own_blocks].astype(F32).reshape(own, width))
    upstream = s["up"][at, :]
    gh = upstream.astype(F32) + unit_backward(gn, inverse, unit_own, gain)
    s["gh_t"][...] = gh.reshape(bins, sub, width).astype(BF)
    gh_back = along((bins, tm - base, in_half), lambda p: s["gh_t"].at[p], s["gh_b"])
    gh_back.start()

    def place(name, index, value):
        part = (value * scale_out).reshape((plane, width // plane, width)).astype(BF)
        s["wg_" + name][:, index] = part

    def plane_sum(name, index, count):
        stack, target = s["wg_" + name], s["rs_" + name]
        at = pl.ds(index, count)
        arrivals = target.at[pl.ds(0, plane - 1), at]
        return Exchange(
            plane, here, in_plane, lambda p: stack.at[p, at], lambda p: target.at[p, at], arrivals, sems()
        )

    def broadcast(group, name, source):
        return along(group, lambda p: s[source], s[name])

    def later_stages(name, result):
        return [
            broadcast(near_group, "near_" + name, "near_src_" + name),
            broadcast(far_group, "far_" + name, "far_src_" + name),
            along(plane_group, lambda p: s["last_src_" + name], result),
        ]

    def add_up(source, count, target):
        s[target][...] = total(s[source], count).astype(s[target].dtype)

    norm = s["n2"][at, :]
    place("time", 0, t_dot(norm, gq))
    place("time", 1, t_dot(norm, gk))
    place("time", 2, t_dot(norm, gv))
    place("time", 3, t_dot(s["o2"][at, :], upstream))
    s["time_gain"][...] = jnp.sum(gn * unit_own, axis=0, keepdims=True) * scale_out
    t_plane = plane_sum("time", 0, 4)
    t_near, t_far, t_last = later_stages("time", sum_ref.at[1])
    t_plane.start()
    gh_back.wait()
    s["gh_l"][...] = swapped(s["gh_b"][...])
    gh_frames = along(freq_group, lambda p: s["gh_l"].at[p], s["gh_f"])
    gh_frames.start()
    t_plane.wait()
    add_up("rs_time", plane, "near_src_time")
    t_near.start()
    gh_frames.wait()

    f_near, f_far, f_last = later_stages("freq", sum_ref.at[0])
    f_planes = [plane_sum("freq", 3, 1), plane_sum("freq", 2, 1), plane_sum("freq", 0, 2)]
    gh32 = s["gh_f"][...].astype(F32).reshape(rows, width)
    gh = gh32.astype(BF)
    go = dot_t(gh, w_ref[3]).astype(BF)
    place("freq", 3, t_dot(s["o1"][...], gh))
    f_planes[0].start()
    gv = jnp.zeros((rows, width), F32)
    for head in range(HEADS):
        gv = gv + dot(s["p1"][head].astype(BF), go * masks[head])
    gv = gv.astype(BF)
    place("freq", 2, t_dot(s["n1"][...], gv))
    f_planes[1].start()
    gq = jnp.zeros((rows, width), F32)
    gk = jnp.zeros((rows, width), F32)
    for head in range(HEADS):
        ds = scores_backward(s["p1"][head], dot_t(s["v1"][...], go * masks[head]))
        gq = gq + t_dot(ds, s["k1"][...] * masks[head])
        gk = gk + dot(ds, s["q1"][...] * masks[head])
    gq, gk = (gq * scale).astype(BF), gk.astype(BF)
    norm = s["n1"][...]
    place("freq", 0, t_dot(norm, gq))
    place("freq", 1, t_dot(norm, gk))
    f_planes[2].start()
    gain = gain_ref[0:1, :]
    inverse, unit_rows = unit(s["x_f"][...].astype(F32).reshape(rows, width))
    gn = dot_t(gq, w_ref[0]) + dot_t(gk, w_ref[1]) + dot_t(gv, w_ref[2])
    gi = gh32 + unit_backward(gn, inverse, unit_rows, gain)
    s["gi_f"][...] = gi.reshape(x_ref.shape).astype(BF)
    gi_back = along(freq_group, lambda p: s["gi_f"].at[p], gi_ref)
    gi_back.start()

    freq_gain = jnp.sum(gn * unit_rows, axis=0, keepdims=True) * scale_out
    s["g_src_plane"][...] = jnp.concatenate([freq_gain, s["time_gain"][...]], axis=0)
    g_plane = broadcast(plane_group, "g_plane", "g_src_plane")
    g_near = broadcast(near_group, "g_near", "g_src_near")
    g_far = broadcast(far_group, "g_far", "g_src_far")
    g_plane.start()

    t_near.wait()
    add_up("near_time", NEAR, "far_src_time")
    t_far.start()
    for stage in f_planes:
        stage.wait()
    add_up("rs_freq", plane, "near_src_freq")
    f_near.start()
    g_plane.wait()
    add_up("g_plane", plane, "g_src_near")
    g_near.start()
    f_near.wait()
    add_up("near_freq", NEAR, "far_src_freq")
    f_far.start()
    g_near.wait()
    add_up("g_near", NEAR, "g_src_far")
    g_far.start()
    t_far.wait()
    add_up("far_time", far, "last_src_time")
    t_last.start()
    f_far.wait()
    add_up("far_freq", far, "last_src_freq")
    f_last.start()
    g_far.wait()
    gain_out[...] = total(s["g_far"], far)
    gi_back.wait()
    t_last.wait()
    f_last.wait()


def finish_kernel(gi_ref, sum_ref, gain_ref, gi_out, w_out, gain_out):
    plane, count, part, width = sum_ref.shape[1:]
    for index in range(count):
        w_out[index] = sum_ref[0, :, index].astype(F32).reshape(plane * part, width)

    @pl.when(pl.program_id(0) == 0)
    def _():
        gi_out[...] = gi_ref[...]
        gain_out[...] = gain_ref[...]


def per_device(features, upstream, weights, gains):
    frames, bins, width = features.shape
    freq_count, tm_count = lax.axis_size("freq"), lax.axis_size("tm")
    rows = bins * freq_count
    scale_out = (frames * tm_count * rows) ** (-0.5)
    shape = jax.ShapeDtypeStruct
    plane, far = tm_count // NEAR * 2, freq_count // 2
    part = width // plane
    span = bins + bins // 2
    all_rows = span * frames

    local = ((frames, bins, width), BF)
    turned = ((bins, frames, width), BF)
    window = ((span, frames, width), BF)
    flat = ((rows, width), BF)
    tall = ((all_rows, width), BF)
    piece = (4, part, width)
    gain = (2, width)
    buffers = dict(
        up_t=turned, up_w=window, x_f=local, n1=flat, q1=flat, k1=flat, v1=flat, o1=flat,
        p1=((HEADS, rows, rows), F32), h_f=local, h_l=local, h_t=turned, h_w=window,
        up=tall, go2=tall, n2=tall, q2=tall, k2=tall, v2=tall, o2=tall, gq2=tall,
        gk2=((all_rows, width), F32), gv2=((all_rows, width), F32),
        gh_t=turned, gh_b=turned, gh_l=local, gh_f=local, gi_f=local,
        time_gain=((1, width), F32),
        g_src_plane=(gain, F32), g_src_near=(gain, F32), g_src_far=(gain, F32),
        g_plane=((plane,) + gain, F32), g_near=((NEAR,) + gain, F32), g_far=((far,) + gain, F32),
    )
    for name in ("freq", "time"):
        buffers["wg_" + name] = ((plane,) + piece, BF)
        buffers["rs_" + name] = ((plane,) + piece, BF)
        buffers["near_src_" + name] = (piece, BF)
        buffers["near_" + name] = ((NEAR,) + piece, BF)
        buffers["far_src_" + name] = (piece, BF)
        buffers["far_" + name] = ((far,) + piece, BF)
        buffers["last_src_" + name] = (piece, BF)
    names = list(buffers)

    outs = pl.pallas_call(
        functools.partial(layer_kernel, scale_out, names),
        out_shape=[
            shape(features.shape, BF),
            shape((2, plane) + piece, BF),
            shape(gain, F32),
        ],
        in_specs=[VMEM_SPEC] * 3 + [pl.BlockSpec(memory_space=pl.ANY)],
        out_specs=[VMEM_SPEC] * 3,
        scratch_shapes=[
            pltpu.VMEM(weights.shape, BF),
            pltpu.SemaphoreType.DMA((48,)),
            pltpu.SemaphoreType.DMA(()),
        ]
        + [pltpu.VMEM(*buffers[name]) for name in names],
        compiler_params=pltpu.CompilerParams(collective_id=0, has_side_effects=True),
        name="layer",
    )(features, upstream, gains, weights)
    whole = [pl.BlockSpec(features.shape, lambda i: (0, 0, 0)), pl.BlockSpec(gain, lambda i: (0, 0))]
    return pl.pallas_call(
        finish_kernel,
        grid=(2,),
        out_shape=[shape(features.shape, BF), shape(weights.shape, F32), shape(gain, F32)],
        in_specs=[
            whole[0],
            pl.BlockSpec((1, plane) + piece, lambda i: (i, 0, 0, 0, 0)),
            whole[1],
        ],
        out_specs=[whole[0], pl.BlockSpec((4, width, width), lambda i: (i, 0, 0)), whole[1]],
        name="finish",
    )(*outs)


def solution(mesh):
    return jax.shard_map(
        per_device,
        mesh=mesh,
        in_specs=(P("tm", "freq", None), P("tm", "freq", None), P(), P()),
        out_specs=(P("tm", "freq", None), P(), P()),
        check_vma=False,
    )
```

```python
import functools

import jax
import jax.numpy as jnp
from jax import lax
from jax.experimental import pallas as pl
from jax.experimental.pallas import tpu as pltpu
from jax.sharding import PartitionSpec as P

HEADS = 4
HALF = 64
EPS = 1e-06
MASKED = -1e30
BF = jnp.bfloat16
F32 = jnp.float32
MESH = pl.DeviceIdType.MESH
NEAR = 4
VMEM_SPEC = pl.BlockSpec(memory_space=pltpu.VMEM)


def dot(a, b):
    return lax.dot_general(a, b, (((1,), (0,)), ((), ())), preferred_element_type=F32)


def dot_t(a, b):
    return lax.dot_general(a, b, (((1,), (1,)), ((), ())), preferred_element_type=F32)


def t_dot(a, b):
    return lax.dot_general(a, b, (((0,), (0,)), ((), ())), preferred_element_type=F32)


def unit(rows):
    inverse = lax.rsqrt(jnp.mean(rows * rows, axis=-1, keepdims=True) + EPS)
    return inverse, rows * inverse


def unit_backward(incoming, inverse, unit_rows, gain):
    scaled = incoming * gain
    mean = jnp.mean(scaled * unit_rows, axis=-1, keepdims=True)
    return inverse * (scaled - unit_rows * mean)


class Exchange:
    def __init__(self, count, me, device_of, source_of, target_of, arrivals, sems):
        self.count, self.me, self.device_of = count, me, device_of
        self.source_of, self.target_of, self.arrivals, self.sems = source_of, target_of, arrivals, sems

    def start(self):
        send_sem, recv_sem = self.sems

        def step(k, carry):
            p = lax.rem(self.me + k, self.count)
            pltpu.make_async_remote_copy(
                src_ref=self.source_of(p),
                dst_ref=self.target_of(self.me),
                send_sem=send_sem,
                recv_sem=recv_sem,
                device_id=self.device_of(p),
                device_id_type=MESH,
            ).start()
            return carry

        lax.fori_loop(1, self.count, step, 0)
        self.target_of(self.me)[...] = self.source_of(self.me)[...]

    def wait(self):
        send_sem, recv_sem = self.sems
        copy = pltpu.make_async_remote_copy(
            src_ref=self.arrivals,
            dst_ref=self.arrivals,
            send_sem=send_sem,
            recv_sem=recv_sem,
            device_id=self.device_of(lax.rem(self.me + 1, self.count)),
            device_id_type=MESH,
        )
        copy.wait_recv()
        copy.wait_send()


class ToTime:
    def __init__(self, bins, me, source, target, sems):
        self.bins, self.halo, self.me = bins, bins // 2, me
        self.mine = lax.div(me, bins)
        self.source, self.target, self.sems = source, target, sems

    def copy(self, source, target, half, device):
        return pltpu.make_async_remote_copy(
            src_ref=source,
            dst_ref=target,
            send_sem=self.sems[half],
            recv_sem=self.sems[2],
            device_id={"tm": device},
            device_id_type=MESH,
        )

    def each_half(self, action):
        for half in range(2):
            needed = (self.me < self.bins + self.halo) if half == 0 else (self.me >= self.halo)
            pl.when(needed)(functools.partial(action, half))

    def start(self):
        def send(half):
            def step(k, carry):
                bin_id = lax.rem(self.me + k, self.bins)
                device = bin_id + self.bins * half

                @pl.when(device != self.me)
                def _():
                    slot = self.target.at[self.me - self.halo * half]
                    self.copy(self.source.at[bin_id], slot, half, device).start()

                return carry

            lax.fori_loop(0, self.bins, step, 0)

        self.each_half(send)
        own = self.me - self.halo * self.mine
        self.target[own] = self.source[self.me - self.bins * self.mine]

    def wait(self):
        other = lax.rem(self.me + 1, 2 * self.bins)
        arrivals = self.target.at[pl.ds(0, self.bins + self.halo - 1)]
        self.copy(arrivals, arrivals, 0, other).wait_recv()

        def sent(half):
            @pl.when(self.mine == half)
            def _():
                left = self.source.at[pl.ds(0, self.bins - 1)]
                self.copy(left, left, half, other).wait_send()

            @pl.when(self.mine != half)
            def _():
                self.copy(self.source, self.source, half, other).wait_send()

        self.each_half(sent)


def total(ref, count):
    return lax.fori_loop(1, count, lambda i, acc: acc + ref[i].astype(F32), ref[0].astype(F32))


def swapped(value):
    return jnp.swapaxes(value.astype(F32), 0, 1).astype(BF)


def head_masks(rows, width):
    lane = lax.broadcasted_iota(jnp.int32, (rows, width), 1) // (width // HEADS)
    return [(lane == head).astype(BF) for head in range(HEADS)]


def weights_of(scores):
    e = jnp.exp(scores - jnp.max(scores, axis=0, keepdims=True))
    return e * (1.0 / jnp.sum(e, axis=0, keepdims=True))


def scores_backward(p, dp):
    return (p * (dp - jnp.sum(dp * p, axis=0, keepdims=True))).astype(BF)


def layer_kernel(
    scale_out, names, x_ref, up_ref, gain_ref, w_hbm, gi_ref, sum_ref, gain_out, w_ref, dma, w_sem, *scratch
):
    s = dict(zip(names, scratch))
    frames, bins, width = x_ref.shape
    scale = (width // HEADS) ** (-0.5)
    tm, freq = lax.axis_index("tm"), lax.axis_index("freq")
    plane, columns = s["wg_time"].shape[0], s["rs_time"].shape[0]
    tm_count, freq_count = columns * NEAR, frames
    core, high = lax.rem(freq, 2), lax.div(freq, 2)
    low, column = lax.rem(tm, NEAR), lax.div(tm, NEAR)
    mine, theirs = core * columns, (1 - core) * columns
    far = freq_count // 2
    rows = bins * freq_count
    base = lax.div(tm, bins) * bins

    def in_freq(p):
        return {"freq": p}

    def in_tm(p):
        return {"tm": p}

    def in_half(p):
        return {"tm": base + p}

    def in_columns(p):
        return {"tm": p * NEAR + low}

    def in_near(p):
        return {"tm": column * NEAR + p, "freq": freq}

    def in_far(p):
        return {"tm": tm, "freq": p * 2 + core}

    used = [0]

    def sems(count=2):
        first = used[0]
        used[0] += count
        return [dma.at[first + i] for i in range(count)]

    def along(group, source_of, target):
        count, me, device_of = group
        arrivals = target.at[pl.ds(0, count - 1)]
        return Exchange(count, me, device_of, source_of, lambda p: target.at[p], arrivals, sems())

    freq_group = (freq_count, freq, in_freq)
    column_group = (columns, column, in_columns)
    near_group = (NEAR, low, in_near)
    far_group = (far, high, in_far)

    barrier = pltpu.get_barrier_semaphore()

    def tell(first, last, peer_of):
        def step(k, carry):
            pl.semaphore_signal(barrier, inc=1, device_id=peer_of(k), device_id_type=MESH)
            return carry

        lax.fori_loop(first, last, step, 0)

    tell(1, freq_count, lambda k: in_freq(lax.rem(freq + k, freq_count)))
    tell(1, tm_count, lambda k: in_tm(lax.rem(tm + k, tm_count)))
    load = pltpu.make_async_copy(w_hbm, w_ref, w_sem)
    load.start()
    s["up_t"][...] = swapped(up_ref[...])
    pl.semaphore_wait(barrier, freq_count - 1 + tm_count - 1)

    to_frames = along(freq_group, lambda p: x_ref.at[p], s["x_f"])
    to_frames.start()
    up_time = ToTime(bins, tm, s["up_t"], s["up_w"], sems(3))
    up_time.start()
    load.wait()
    to_frames.wait()

    masks = head_masks(rows, width)
    gain = gain_ref[0:1, :]
    x = s["x_f"][...].astype(F32).reshape(rows, width)
    _, unit_rows = unit(x)
    norm = (unit_rows * gain).astype(BF)
    s["n1"][...] = norm
    s["q1"][...] = (dot(norm, w_ref[0]).astype(BF) * scale).astype(BF)
    s["k1"][...] = dot(norm, w_ref[1]).astype(BF)
    s["v1"][...] = dot(norm, w_ref[2]).astype(BF)
    mixed = jnp.zeros((rows, width), F32)
    for head in range(HEADS):
        p = weights_of(dot_t(s["k1"][...], s["q1"][...] * masks[head]))
        s["p1"][head] = p
        mixed = mixed + t_dot(p.astype(BF), s["v1"][...] * masks[head])
    s["o1"][...] = mixed.astype(BF)
    hidden = x + dot(s["o1"][...], w_ref[3])
    s["h_f"][...] = hidden.reshape(x_ref.shape).astype(BF)
    h_back = along(freq_group, lambda p: s["h_f"].at[p], s["h_l"])
    h_back.start()

    up_time.wait()
    blocks, sub = s["up_w"].shape[:2]
    all_rows, own = blocks * sub, bins * sub
    s["up"][...] = s["up_w"][...].astype(F32).reshape(all_rows, width).astype(BF)
    s["go2"][...] = dot_t(s["up"][...], w_ref[7]).astype(BF)
    s["gk2"][...] = jnp.zeros_like(s["gk2"])
    s["gv2"][...] = jnp.zeros_like(s["gv2"])
    h_back.wait()
    s["h_t"][...] = swapped(s["h_l"][...])
    h_time = ToTime(bins, tm, s["h_t"], s["h_w"], sems(3))
    h_time.start()
    h_time.wait()

    gain = gain_ref[1:2, :]
    _, unit_rows = unit(s["h_w"][...].astype(F32).reshape(all_rows, width))
    norm = (unit_rows * gain).astype(BF)
    s["n2"][...] = norm
    s["q2"][...] = (dot(norm, w_ref[4]).astype(BF) * scale).astype(BF)
    s["k2"][...] = dot(norm, w_ref[5]).astype(BF)
    s["v2"][...] = dot(norm, w_ref[6]).astype(BF)
    queries, keys = 2 * HALF, 4 * HALF
    offset = lax.broadcasted_iota(jnp.int32, (keys, queries), 0) - lax.broadcasted_iota(
        jnp.int32, (keys, queries), 1
    )

    def block(i, carry):
        q_at = pl.ds(pl.multiple_of(i * queries, queries), queries)
        k_at = pl.ds(pl.multiple_of(i * HALF, HALF), keys)
        q, go, k, v = s["q2"][q_at, :], s["go2"][q_at, :], s["k2"][k_at, :], s["v2"][k_at, :]
        distance = offset - HALF * i
        allowed = (distance >= -HALF) & (distance < HALF)
        key_masks, query_masks = head_masks(keys, width), head_masks(queries, width)
        mixed = jnp.zeros((queries, width), F32)
        gq = jnp.zeros((queries, width), F32)
        gk = jnp.zeros((keys, width), F32)
        gv = jnp.zeros((keys, width), F32)
        for head in range(HEADS):
            q_head, go_head = q * query_masks[head], go * query_masks[head]
            p = weights_of(jnp.where(allowed, dot_t(k, q_head), MASKED))
            p_half = p.astype(BF)
            ds = scores_backward(p, dot_t(v, go_head))
            mixed = mixed + t_dot(p_half, v * key_masks[head])
            gq = gq + t_dot(ds, k * key_masks[head])
            gk = gk + dot(ds, q_head)
            gv = gv + dot(p_half, go_head)
        s["o2"][q_at, :] = mixed.astype(BF)
        s["gq2"][q_at, :] = (gq * scale).astype(BF)
        s["gk2"][k_at, :] += gk
        s["gv2"][k_at, :] += gv
        return carry

    lax.fori_loop(0, all_rows // queries, block, 0)

    half = lax.div(tm, bins)
    first = pl.multiple_of(half * (own // 2), own // 2)
    at = pl.ds(first, own)
    gq, gk, gv = s["gq2"][at, :], s["gk2"][at, :].astype(BF), s["gv2"][at, :].astype(BF)
    gn = dot_t(gq, w_ref[4]) + dot_t(gk, w_ref[5]) + dot_t(gv, w_ref[6])
    own_blocks = pl.ds(half * (bins // 2), bins)
    inverse, unit_own = unit(s["h_w"][own_blocks].astype(F32).reshape(own, width))
    upstream = s["up"][at, :]
    gh = upstream.astype(F32) + unit_backward(gn, inverse, unit_own, gain)
    s["gh_t"][...] = gh.reshape(bins, sub, width).astype(BF)
    gh_back = along((bins, tm - base, in_half), lambda p: s["gh_t"].at[p], s["gh_b"])
    gh_back.start()

    def place(name, index, value):
        part = (value * scale_out).reshape((plane, width // plane, width)).astype(BF)
        s["wg_" + name][:, index] = part

    def to_partner(source, target):
        send_sem, recv_sem = sems()
        return pltpu.make_async_remote_copy(
            src_ref=source,
            dst_ref=target,
            send_sem=send_sem,
            recv_sem=recv_sem,
            device_id={"freq": freq + 1 - 2 * core},
            device_id_type=MESH,
        )

    def halve(name, index, count):
        at = pl.ds(index, count)
        return to_partner(s["wg_" + name].at[pl.ds(theirs, columns), at], s["pair_" + name].at[:, at])

    def add_pair(name, index, count):
        at = pl.ds(index, count)
        own = s["wg_" + name][pl.ds(mine, columns), at].astype(F32)
        s["both_" + name][:, at] = (own + s["pair_" + name][:, at].astype(F32)).astype(BF)

    def broadcast(group, name, source):
        return along(group, lambda p: s[source], s[name])

    def later_stages(name, result):
        part = result.at[pl.ds(mine, columns)]
        return [
            along(column_group, lambda p: s["both_" + name].at[p], s["rs_" + name]),
            broadcast(near_group, "near_" + name, "near_src_" + name),
            broadcast(far_group, "far_" + name, "far_src_" + name),
            along(column_group, lambda p: s["last_src_" + name], part),
            to_partner(part, part),
        ]

    def add_up(source, count, target):
        s[target][...] = total(s[source], count).astype(s[target].dtype)

    norm = s["n2"][at, :]
    place("time", 0, t_dot(norm, gq))
    place("time", 1, t_dot(norm, gk))
    place("time", 2, t_dot(norm, gv))
    place("time", 3, t_dot(s["o2"][at, :], upstream))
    s["time_gain"][...] = jnp.sum(gn * unit_own, axis=0, keepdims=True) * scale_out
    t_pair = halve("time", 0, 4)
    t_plane, t_near, t_far, t_last, t_out = later_stages("time", sum_ref.at[1])
    t_pair.start()
    t_pair.wait()
    add_pair("time", 0, 4)
    t_plane.start()
    gh_back.wait()
    s["gh_l"][...] = swapped(s["gh_b"][...])
    gh_frames = along(freq_group, lambda p: s["gh_l"].at[p], s["gh_f"])
    gh_frames.start()
    t_plane.wait()
    add_up("rs_time", columns, "near_src_time")
    t_near.start()
    t_near.wait()
    add_up("near_time", NEAR, "far_src_time")
    t_far.start()
    gh_frames.wait()

    f_pairs = [halve("freq", 3, 2), halve("freq", 0, 3)]
    f_plane, f_near, f_far, f_last, f_out = later_stages("freq", sum_ref.at[0])
    gh32 = s["gh_f"][...].astype(F32).reshape(rows, width)
    gh = gh32.astype(BF)
    go = dot_t(gh, w_ref[3]).astype(BF)
    place("freq", 4, t_dot(s["o1"][...], gh))
    gv = jnp.zeros((rows, width), F32)
    for head in range(HEADS):
        gv = gv + dot(s["p1"][head].astype(BF), go * masks[head])
    gv = gv.astype(BF)
    place("freq", 3, t_dot(s["n1"][...], gv))
    f_pairs[0].start()
    gq = jnp.zeros((rows, width), F32)
    gk = jnp.zeros((rows, width), F32)
    for head in range(HEADS):
        ds = scores_backward(s["p1"][head], dot_t(s["v1"][...], go * masks[head]))
        gq = gq + t_dot(ds, s["k1"][...] * masks[head])
        gk = gk + dot(ds, s["q1"][...] * masks[head])
    gq, gk = (gq * scale).astype(BF), gk.astype(BF)
    norm = s["n1"][...]
    place("freq", 1, t_dot(norm, gq))
    place("freq", 2, t_dot(norm, gk))
    gain = gain_ref[0:1, :]
    inverse, unit_rows = unit(s["x_f"][...].astype(F32).reshape(rows, width))
    gn = dot_t(gq, w_ref[0]) + dot_t(gk, w_ref[1]) + dot_t(gv, w_ref[2])
    freq_gain = jnp.sum(gn * unit_rows, axis=0, keepdims=True) * scale_out
    gain_rows = jnp.concatenate(
        [freq_gain, s["time_gain"][...], jnp.zeros((width // plane - 2, width), F32)], axis=0
    )
    s["wg_freq"][:, 0] = jnp.broadcast_to(gain_rows[None], (plane,) + gain_rows.shape).astype(BF)
    f_pairs[1].start()
    f_pairs[0].wait()
    add_pair("freq", 3, 2)
    gi = gh32 + unit_backward(gn, inverse, unit_rows, gain)
    s["gi_f"][...] = gi.reshape(x_ref.shape).astype(BF)
    f_pairs[1].wait()
    add_pair("freq", 0, 3)
    f_plane.start()
    gi_back = along(freq_group, lambda p: s["gi_f"].at[p], gi_ref)
    gi_back.start()

    f_plane.wait()
    add_up("rs_freq", columns, "near_src_freq")
    f_near.start()
    t_far.wait()
    add_up("far_time", far, "last_src_time")
    t_last.start()
    f_near.wait()
    add_up("near_freq", NEAR, "far_src_freq")
    f_far.start()
    t_last.wait()
    t_out.start()
    f_far.wait()
    sums = total(s["far_freq"], far)
    s["last_src_freq"][...] = sums[1:].astype(BF)
    f_last.start()
    gain_out[...] = sums[0, 0:2]
    gi_back.wait()
    f_last.wait()
    f_out.start()
    t_out.wait()
    f_out.wait()


def finish_kernel(gi_ref, sum_ref, gain_ref, gi_out, w_out, gain_out):
    plane, count, part, width = sum_ref.shape[1:]
    for index in range(count):
        w_out[index] = sum_ref[0, :, index].astype(F32).reshape(plane * part, width)

    @pl.when(pl.program_id(0) == 0)
    def _():
        gi_out[...] = gi_ref[...]
        gain_out[...] = gain_ref[...]


def per_device(features, upstream, weights, gains):
    frames, bins, width = features.shape
    freq_count, tm_count = lax.axis_size("freq"), lax.axis_size("tm")
    rows = bins * freq_count
    scale_out = (frames * tm_count * rows) ** (-0.5)
    shape = jax.ShapeDtypeStruct
    plane, far = tm_count // NEAR * 2, freq_count // 2
    part = width // plane
    span = bins + bins // 2
    all_rows = span * frames

    local = ((frames, bins, width), BF)
    turned = ((bins, frames, width), BF)
    window = ((span, frames, width), BF)
    flat = ((rows, width), BF)
    tall = ((all_rows, width), BF)
    piece = (4, part, width)
    gain = (2, width)
    buffers = dict(
        up_t=turned, up_w=window, x_f=local, n1=flat, q1=flat, k1=flat, v1=flat, o1=flat,
        p1=((HEADS, rows, rows), F32), h_f=local, h_l=local, h_t=turned, h_w=window,
        up=tall, go2=tall, n2=tall, q2=tall, k2=tall, v2=tall, o2=tall, gq2=tall,
        gk2=((all_rows, width), F32), gv2=((all_rows, width), F32),
        gh_t=turned, gh_b=turned, gh_l=local, gh_f=local, gi_f=local,
        time_gain=((1, width), F32),
    )
    for name, pieces in (("freq", 5), ("time", 4)):
        stack = (pieces, part, width)
        buffers["wg_" + name] = ((plane,) + stack, BF)
        for step in ("pair_", "both_", "rs_"):
            buffers[step + name] = ((plane // 2,) + stack, BF)
        buffers["near_src_" + name] = (stack, BF)
        buffers["near_" + name] = ((NEAR,) + stack, BF)
        buffers["far_src_" + name] = (stack, BF)
        buffers["far_" + name] = ((far,) + stack, BF)
        buffers["last_src_" + name] = (piece, BF)
    names = list(buffers)

    outs = pl.pallas_call(
        functools.partial(layer_kernel, scale_out, names),
        out_shape=[
            shape(features.shape, BF),
            shape((2, plane) + piece, BF),
            shape(gain, F32),
        ],
        in_specs=[VMEM_SPEC] * 3 + [pl.BlockSpec(memory_space=pl.ANY)],
        out_specs=[VMEM_SPEC] * 3,
        scratch_shapes=[
            pltpu.VMEM(weights.shape, BF),
            pltpu.SemaphoreType.DMA((48,)),
            pltpu.SemaphoreType.DMA(()),
        ]
        + [pltpu.VMEM(*buffers[name]) for name in names],
        compiler_params=pltpu.CompilerParams(collective_id=0, has_side_effects=True),
        name="layer",
    )(features, upstream, gains, weights)
    whole = [pl.BlockSpec(features.shape, lambda i: (0, 0, 0)), pl.BlockSpec(gain, lambda i: (0, 0))]
    return pl.pallas_call(
        finish_kernel,
        grid=(2,),
        out_shape=[shape(features.shape, BF), shape(weights.shape, F32), shape(gain, F32)],
        in_specs=[
            whole[0],
            pl.BlockSpec((1, plane) + piece, lambda i: (i, 0, 0, 0, 0)),
            whole[1],
        ],
        out_specs=[whole[0], pl.BlockSpec((4, width, width), lambda i: (i, 0, 0)), whole[1]],
        name="finish",
    )(*outs)


def solution(mesh):
    return jax.shard_map(
        per_device,
        mesh=mesh,
        in_specs=(P("tm", "freq", None), P("tm", "freq", None), P(), P()),
        out_specs=(P("tm", "freq", None), P(), P()),
        check_vma=False,
    )
```

```python
import functools

import jax
import jax.numpy as jnp
from jax import lax
from jax.experimental import pallas as pl
from jax.experimental.pallas import tpu as pltpu
from jax.sharding import PartitionSpec as P

HEADS = 4
HALF = 64
EPS = 1e-06
MASKED = -1e30
BF = jnp.bfloat16
F32 = jnp.float32
MESH = pl.DeviceIdType.MESH
SEMAPHORES = 42
NEAR = 4
VMEM_SPEC = pl.BlockSpec(memory_space=pltpu.VMEM)


def dot(a, b):
    return lax.dot_general(a, b, (((1,), (0,)), ((), ())), preferred_element_type=F32)


def dot_t(a, b):
    return lax.dot_general(a, b, (((1,), (1,)), ((), ())), preferred_element_type=F32)


def t_dot(a, b):
    return lax.dot_general(a, b, (((0,), (0,)), ((), ())), preferred_element_type=F32)


def unit(rows):
    inverse = lax.rsqrt(jnp.mean(rows * rows, axis=-1, keepdims=True) + EPS)
    return inverse, rows * inverse


def unit_backward(incoming, inverse, unit_rows, gain):
    scaled = incoming * gain
    mean = jnp.mean(scaled * unit_rows, axis=-1, keepdims=True)
    return inverse * (scaled - unit_rows * mean)


class Exchange:
    def __init__(self, count, me, device_of, source_of, target_of, arrivals, sems):
        self.count, self.me, self.device_of = count, me, device_of
        self.source_of, self.target_of, self.arrivals, self.sems = source_of, target_of, arrivals, sems

    def start(self):
        send_sem, recv_sem = self.sems

        def step(k, carry):
            p = lax.rem(self.me + k, self.count)
            pltpu.make_async_remote_copy(
                src_ref=self.source_of(p),
                dst_ref=self.target_of(self.me),
                send_sem=send_sem,
                recv_sem=recv_sem,
                device_id=self.device_of(p),
                device_id_type=MESH,
            ).start()
            return carry

        lax.fori_loop(1, self.count, step, 0)
        self.target_of(self.me)[...] = self.source_of(self.me)[...]

    def wait(self):
        send_sem, recv_sem = self.sems
        copy = pltpu.make_async_remote_copy(
            src_ref=self.arrivals,
            dst_ref=self.arrivals,
            send_sem=send_sem,
            recv_sem=recv_sem,
            device_id=self.device_of(lax.rem(self.me + 1, self.count)),
            device_id_type=MESH,
        )
        copy.wait_recv()
        copy.wait_send()


class ToTime:
    def __init__(self, bins, me, source, target, sems):
        self.bins, self.halo, self.me = bins, bins // 2, me
        self.mine = lax.div(me, bins)
        self.source, self.target, self.sems = source, target, sems

    def copy(self, source, target, half, device):
        return pltpu.make_async_remote_copy(
            src_ref=source,
            dst_ref=target,
            send_sem=self.sems[half],
            recv_sem=self.sems[2],
            device_id={"tm": device},
            device_id_type=MESH,
        )

    def each_half(self, action):
        for half in range(2):
            needed = (self.me < self.bins + self.halo) if half == 0 else (self.me >= self.halo)
            pl.when(needed)(functools.partial(action, half))

    def start(self):
        def send(half):
            def step(k, carry):
                bin_id = lax.rem(self.me + k, self.bins)
                device = bin_id + self.bins * half

                @pl.when(device != self.me)
                def _():
                    slot = self.target.at[self.me - self.halo * half]
                    self.copy(self.source.at[bin_id], slot, half, device).start()

                return carry

            lax.fori_loop(0, self.bins, step, 0)

        self.each_half(send)
        own = self.me - self.halo * self.mine
        self.target[own] = self.source[self.me - self.bins * self.mine]

    def wait(self):
        other = lax.rem(self.me + 1, 2 * self.bins)
        arrivals = self.target.at[pl.ds(0, self.bins + self.halo - 1)]
        self.copy(arrivals, arrivals, 0, other).wait_recv()

        def sent(half):
            @pl.when(self.mine == half)
            def _():
                left = self.source.at[pl.ds(0, self.bins - 1)]
                self.copy(left, left, half, other).wait_send()

            @pl.when(self.mine != half)
            def _():
                self.copy(self.source, self.source, half, other).wait_send()

        self.each_half(sent)


def total(ref, count):
    return lax.fori_loop(1, count, lambda i, acc: acc + ref[i].astype(F32), ref[0].astype(F32))


def swapped(value):
    return jnp.swapaxes(value.astype(F32), 0, 1).astype(BF)


def head_masks(rows, width):
    lane = lax.broadcasted_iota(jnp.int32, (rows, width), 1) // (width // HEADS)
    return [(lane == head).astype(BF) for head in range(HEADS)]


def weights_of(scores):
    e = jnp.exp(scores - jnp.max(scores, axis=0, keepdims=True))
    return e * (1.0 / jnp.sum(e, axis=0, keepdims=True))


def scores_backward(p, dp):
    return (p * (dp - jnp.sum(dp * p, axis=0, keepdims=True))).astype(BF)


def layer_kernel(
    scale_out, names, x_hbm, up_hbm, gain_hbm, w_hbm, gi_ref, sum_ref, gain_out,
    x_ref, up_ref, gain_ref, w_ref, dma, load_sem, *scratch
):
    s = dict(zip(names, scratch))
    frames, bins, width = x_ref.shape
    scale = (width // HEADS) ** (-0.5)
    tm, freq = lax.axis_index("tm"), lax.axis_index("freq")
    plane, columns = s["wg_time"].shape[0], s["rs_time"].shape[0]
    tm_count, freq_count = columns * NEAR, frames
    core, high = lax.rem(freq, 2), lax.div(freq, 2)
    low, column = lax.rem(tm, NEAR), lax.div(tm, NEAR)
    mine, theirs = core * columns, (1 - core) * columns
    far = freq_count // 2
    rows = bins * freq_count
    base = lax.div(tm, bins) * bins

    def in_freq(p):
        return {"freq": p}

    def in_tm(p):
        return {"tm": p}

    def in_half(p):
        return {"tm": base + p}

    def in_columns(p):
        return {"tm": p * NEAR + low}

    def in_near(p):
        return {"tm": column * NEAR + p, "freq": freq}

    def in_far(p):
        return {"tm": tm, "freq": p * 2 + core}

    used = [0]

    def sems(count=2):
        first = used[0]
        used[0] += count
        return [dma.at[first + i] for i in range(count)]

    def along(group, source_of, target):
        count, me, device_of = group
        arrivals = target.at[pl.ds(0, count - 1)]
        return Exchange(count, me, device_of, source_of, lambda p: target.at[p], arrivals, sems())

    freq_group = (freq_count, freq, in_freq)
    column_group = (columns, column, in_columns)
    near_group = (NEAR, low, in_near)
    far_group = (far, high, in_far)

    pairs = ((x_hbm, x_ref), (up_hbm, up_ref), (gain_hbm, gain_ref), (w_hbm, w_ref))
    loads = [pltpu.make_async_copy(a, b, load_sem.at[i]) for i, (a, b) in enumerate(pairs)]
    for load in loads:
        load.start()

    barrier = pltpu.get_barrier_semaphore()

    def tell(first, last, peer_of):
        def step(k, carry):
            pl.semaphore_signal(barrier, inc=1, device_id=peer_of(k), device_id_type=MESH)
            return carry

        lax.fori_loop(first, last, step, 0)

    tell(1, freq_count, lambda k: in_freq(lax.rem(freq + k, freq_count)))
    tell(1, tm_count, lambda k: in_tm(lax.rem(tm + k, tm_count)))
    for load in loads[:3]:
        load.wait()
    s["up_t"][...] = swapped(up_ref[...])
    pl.semaphore_wait(barrier, freq_count - 1 + tm_count - 1)

    to_frames = along(freq_group, lambda p: x_ref.at[p], s["x_f"])
    to_frames.start()
    up_time = ToTime(bins, tm, s["up_t"], s["up_w"], sems(3))
    up_time.start()
    loads[3].wait()
    to_frames.wait()

    masks = head_masks(rows, width)
    gain = gain_ref[0:1, :]
    x = s["x_f"][...].astype(F32).reshape(rows, width)
    _, unit_rows = unit(x)
    norm = (unit_rows * gain).astype(BF)
    s["n1"][...] = norm
    s["q1"][...] = (dot(norm, w_ref[0]).astype(BF) * scale).astype(BF)
    s["k1"][...] = dot(norm, w_ref[1]).astype(BF)
    s["v1"][...] = dot(norm, w_ref[2]).astype(BF)
    mixed = jnp.zeros((rows, width), F32)
    for head in range(HEADS):
        p = weights_of(dot_t(s["k1"][...], s["q1"][...] * masks[head]))
        s["p1"][head] = p
        mixed = mixed + t_dot(p.astype(BF), s["v1"][...] * masks[head])
    s["o1"][...] = mixed.astype(BF)
    hidden = x + dot(s["o1"][...], w_ref[3])
    s["h_f"][...] = hidden.reshape(x_ref.shape).astype(BF)
    h_back = along(freq_group, lambda p: s["h_f"].at[p], s["h_l"])
    h_back.start()

    up_time.wait()
    blocks, sub = s["up_w"].shape[:2]
    all_rows, own = blocks * sub, bins * sub
    s["up"][...] = s["up_w"][...].astype(F32).reshape(all_rows, width).astype(BF)
    s["go2"][...] = dot_t(s["up"][...], w_ref[7]).astype(BF)
    s["gk2"][...] = jnp.zeros_like(s["gk2"])
    s["gv2"][...] = jnp.zeros_like(s["gv2"])
    h_back.wait()
    s["h_t"][...] = swapped(s["h_l"][...])
    h_time = ToTime(bins, tm, s["h_t"], s["h_w"], sems(3))
    h_time.start()
    h_time.wait()

    gain = gain_ref[1:2, :]
    _, unit_rows = unit(s["h_w"][...].astype(F32).reshape(all_rows, width))
    norm = (unit_rows * gain).astype(BF)
    s["n2"][...] = norm
    s["q2"][...] = (dot(norm, w_ref[4]).astype(BF) * scale).astype(BF)
    s["k2"][...] = dot(norm, w_ref[5]).astype(BF)
    s["v2"][...] = dot(norm, w_ref[6]).astype(BF)
    queries, keys = 2 * HALF, 4 * HALF
    offset = lax.broadcasted_iota(jnp.int32, (keys, queries), 0) - lax.broadcasted_iota(
        jnp.int32, (keys, queries), 1
    )

    def block(i, carry):
        q_at = pl.ds(pl.multiple_of(i * queries, queries), queries)
        k_at = pl.ds(pl.multiple_of(i * HALF, HALF), keys)
        q, go, k, v = s["q2"][q_at, :], s["go2"][q_at, :], s["k2"][k_at, :], s["v2"][k_at, :]
        distance = offset - HALF * i
        allowed = (distance >= -HALF) & (distance < HALF)
        key_masks, query_masks = head_masks(keys, width), head_masks(queries, width)
        mixed = jnp.zeros((queries, width), F32)
        gq = jnp.zeros((queries, width), F32)
        gk = jnp.zeros((keys, width), F32)
        gv = jnp.zeros((keys, width), F32)
        for head in range(HEADS):
            q_head, go_head = q * query_masks[head], go * query_masks[head]
            p = weights_of(jnp.where(allowed, dot_t(k, q_head), MASKED))
            p_half = p.astype(BF)
            ds = scores_backward(p, dot_t(v, go_head))
            mixed = mixed + t_dot(p_half, v * key_masks[head])
            gq = gq + t_dot(ds, k * key_masks[head])
            gk = gk + dot(ds, q_head)
            gv = gv + dot(p_half, go_head)
        s["o2"][q_at, :] = mixed.astype(BF)
        s["gq2"][q_at, :] = (gq * scale).astype(BF)
        s["gk2"][k_at, :] += gk
        s["gv2"][k_at, :] += gv
        return carry

    lax.fori_loop(0, all_rows // queries, block, 0)

    half = lax.div(tm, bins)
    first = pl.multiple_of(half * (own // 2), own // 2)
    at = pl.ds(first, own)
    gq, gk, gv = s["gq2"][at, :], s["gk2"][at, :].astype(BF), s["gv2"][at, :].astype(BF)
    gn = dot_t(gq, w_ref[4]) + dot_t(gk, w_ref[5]) + dot_t(gv, w_ref[6])
    own_blocks = pl.ds(half * (bins // 2), bins)
    inverse, unit_own = unit(s["h_w"][own_blocks].astype(F32).reshape(own, width))
    upstream = s["up"][at, :]
    gh = upstream.astype(F32) + unit_backward(gn, inverse, unit_own, gain)
    s["gh_t"][...] = gh.reshape(bins, sub, width).astype(BF)
    gh_back = along((bins, tm - base, in_half), lambda p: s["gh_t"].at[p], s["gh_b"])
    gh_back.start()

    def place(name, index, value):
        part = (value * scale_out).reshape((plane, width // plane, width)).astype(BF)
        s["wg_" + name][:, index] = part

    def to_partner(source, target):
        send_sem, recv_sem = sems()
        return pltpu.make_async_remote_copy(
            src_ref=source,
            dst_ref=target,
            send_sem=send_sem,
            recv_sem=recv_sem,
            device_id={"freq": freq + 1 - 2 * core},
            device_id_type=MESH,
        )

    def halve(name, index, count):
        at = pl.ds(index, count)
        return to_partner(s["wg_" + name].at[pl.ds(theirs, columns), at], s["pair_" + name].at[:, at])

    def add_pair(name, index, count):
        at = pl.ds(index, count)
        own = s["wg_" + name][pl.ds(mine, columns), at].astype(F32)
        s["both_" + name][:, at] = (own + s["pair_" + name][:, at].astype(F32)).astype(BF)

    def broadcast(group, name, source):
        return along(group, lambda p: s[source], s[name])

    def later_stages(name, result):
        part = result.at[pl.ds(mine, columns)]
        return [
            along(column_group, lambda p: s["both_" + name].at[p], s["rs_" + name]),
            broadcast(near_group, "near_" + name, "near_src_" + name),
            broadcast(far_group, "far_" + name, "far_src_" + name),
            along(column_group, lambda p: s["last_src_" + name], part),
            to_partner(part, part),
        ]

    def add_up(source, count, target):
        s[target][...] = total(s[source], count).astype(s[target].dtype)

    norm = s["n2"][at, :]
    place("time", 0, t_dot(norm, gq))
    place("time", 1, t_dot(norm, gk))
    place("time", 2, t_dot(norm, gv))
    place("time", 3, t_dot(s["o2"][at, :], upstream))
    s["time_gain"][...] = jnp.sum(gn * unit_own, axis=0, keepdims=True) * scale_out
    t_pair = halve("time", 0, 4)
    t_plane, t_near, t_far, t_last, t_out = later_stages("time", sum_ref.at[1])
    t_pair.start()
    t_pair.wait()
    add_pair("time", 0, 4)
    t_plane.start()
    gh_back.wait()
    s["gh_l"][...] = swapped(s["gh_b"][...])
    gh_frames = along(freq_group, lambda p: s["gh_l"].at[p], s["gh_f"])
    gh_frames.start()
    t_plane.wait()
    add_up("rs_time", columns, "near_src_time")
    t_near.start()
    t_near.wait()
    add_up("near_time", NEAR, "far_src_time")
    t_far.start()
    gh_frames.wait()

    f_pairs = [halve("freq", 3, 2), halve("freq", 0, 3)]
    f_plane, f_near, f_far, f_last, f_out = later_stages("freq", sum_ref.at[0])
    gh32 = s["gh_f"][...].astype(F32).reshape(rows, width)
    gh = gh32.astype(BF)
    go = dot_t(gh, w_ref[3]).astype(BF)
    place("freq", 4, t_dot(s["o1"][...], gh))
    gv = jnp.zeros((rows, width), F32)
    for head in range(HEADS):
        gv = gv + dot(s["p1"][head].astype(BF), go * masks[head])
    gv = gv.astype(BF)
    place("freq", 3, t_dot(s["n1"][...], gv))
    f_pairs[0].start()
    gq = jnp.zeros((rows, width), F32)
    gk = jnp.zeros((rows, width), F32)
    for head in range(HEADS):
        ds = scores_backward(s["p1"][head], dot_t(s["v1"][...], go * masks[head]))
        gq = gq + t_dot(ds, s["k1"][...] * masks[head])
        gk = gk + dot(ds, s["q1"][...] * masks[head])
    gq, gk = (gq * scale).astype(BF), gk.astype(BF)
    norm = s["n1"][...]
    place("freq", 1, t_dot(norm, gq))
    place("freq", 2, t_dot(norm, gk))
    gain = gain_ref[0:1, :]
    inverse, unit_rows = unit(s["x_f"][...].astype(F32).reshape(rows, width))
    gn = dot_t(gq, w_ref[0]) + dot_t(gk, w_ref[1]) + dot_t(gv, w_ref[2])
    freq_gain = jnp.sum(gn * unit_rows, axis=0, keepdims=True) * scale_out
    gain_rows = jnp.concatenate(
        [freq_gain, s["time_gain"][...], jnp.zeros((width // plane - 2, width), F32)], axis=0
    )
    s["wg_freq"][:, 0] = jnp.broadcast_to(gain_rows[None], (plane,) + gain_rows.shape).astype(BF)
    f_pairs[1].start()
    f_pairs[0].wait()
    add_pair("freq", 3, 2)
    gi = gh32 + unit_backward(gn, inverse, unit_rows, gain)
    s["gi_f"][...] = gi.reshape(x_ref.shape).astype(BF)
    f_pairs[1].wait()
    add_pair("freq", 0, 3)
    f_plane.start()
    gi_back = along(freq_group, lambda p: s["gi_f"].at[p], gi_ref)
    gi_back.start()

    f_plane.wait()
    add_up("rs_freq", columns, "near_src_freq")
    f_near.start()
    t_far.wait()
    add_up("far_time", far, "last_src_time")
    t_last.start()
    f_near.wait()
    add_up("near_freq", NEAR, "far_src_freq")
    f_far.start()
    t_last.wait()
    t_out.start()
    f_far.wait()
    sums = total(s["far_freq"], far)
    s["last_src_freq"][...] = sums[1:].astype(BF)
    f_last.start()
    gain_out[...] = sums[0, 0:2]
    gi_back.wait()
    f_last.wait()
    f_out.start()
    t_out.wait()
    f_out.wait()
    assert used[0] <= SEMAPHORES, used


def finish_kernel(gi_ref, sum_ref, gain_ref, gi_out, w_out, gain_out):
    plane, count, part, width = sum_ref.shape[1:]
    for index in range(count):
        w_out[index] = sum_ref[0, :, index].astype(F32).reshape(plane * part, width)

    @pl.when(pl.program_id(0) == 0)
    def _():
        gi_out[...] = gi_ref[...]
        gain_out[...] = gain_ref[...]


def per_device(features, upstream, weights, gains):
    frames, bins, width = features.shape
    freq_count, tm_count = lax.axis_size("freq"), lax.axis_size("tm")
    rows = bins * freq_count
    scale_out = (frames * tm_count * rows) ** (-0.5)
    shape = jax.ShapeDtypeStruct
    plane, far = tm_count // NEAR * 2, freq_count // 2
    part = width // plane
    span = bins + bins // 2
    all_rows = span * frames

    local = ((frames, bins, width), BF)
    turned = ((bins, frames, width), BF)
    window = ((span, frames, width), BF)
    flat = ((rows, width), BF)
    tall = ((all_rows, width), BF)
    piece = (4, part, width)
    gain = (2, width)
    buffers = dict(
        up_t=turned, up_w=window, x_f=local, n1=flat, q1=flat, k1=flat, v1=flat, o1=flat,
        p1=((HEADS, rows, rows), F32), h_f=local, h_l=local, h_t=turned, h_w=window,
        up=tall, go2=tall, n2=tall, q2=tall, k2=tall, v2=tall, o2=tall, gq2=tall,
        gk2=((all_rows, width), F32), gv2=((all_rows, width), F32),
        gh_t=turned, gh_b=turned, gh_l=local, gh_f=local, gi_f=local,
        time_gain=((1, width), F32),
    )
    for name, pieces in (("freq", 5), ("time", 4)):
        stack = (pieces, part, width)
        buffers["wg_" + name] = ((plane,) + stack, BF)
        for step in ("pair_", "both_", "rs_"):
            buffers[step + name] = ((plane // 2,) + stack, BF)
        buffers["near_src_" + name] = (stack, BF)
        buffers["near_" + name] = ((NEAR,) + stack, BF)
        buffers["far_src_" + name] = (stack, BF)
        buffers["far_" + name] = ((far,) + stack, BF)
        buffers["last_src_" + name] = (piece, BF)
    names = list(buffers)

    outs = pl.pallas_call(
        functools.partial(layer_kernel, scale_out, names),
        out_shape=[
            shape(features.shape, BF),
            shape((2, plane) + piece, BF),
            shape(gain, F32),
        ],
        in_specs=[pl.BlockSpec(memory_space=pl.ANY)] * 4,
        out_specs=[VMEM_SPEC] * 3,
        scratch_shapes=[
            pltpu.VMEM(features.shape, BF),
            pltpu.VMEM(upstream.shape, BF),
            pltpu.VMEM(gain, F32),
            pltpu.VMEM(weights.shape, BF),
            pltpu.SemaphoreType.DMA((SEMAPHORES,)),
            pltpu.SemaphoreType.DMA((4,)),
        ]
        + [pltpu.VMEM(*buffers[name]) for name in names],
        compiler_params=pltpu.CompilerParams(collective_id=0, has_side_effects=True),
        name="layer",
    )(features, upstream, gains, weights)
    whole = [pl.BlockSpec(features.shape, lambda i: (0, 0, 0)), pl.BlockSpec(gain, lambda i: (0, 0))]
    return pl.pallas_call(
        finish_kernel,
        grid=(2,),
        out_shape=[shape(features.shape, BF), shape(weights.shape, F32), shape(gain, F32)],
        in_specs=[
            whole[0],
            pl.BlockSpec((1, plane) + piece, lambda i: (i, 0, 0, 0, 0)),
            whole[1],
        ],
        out_specs=[whole[0], pl.BlockSpec((4, width, width), lambda i: (i, 0, 0)), whole[1]],
        name="finish",
    )(*outs)


def solution(mesh):
    return jax.shard_map(
        per_device,
        mesh=mesh,
        in_specs=(P("tm", "freq", None), P("tm", "freq", None), P(), P()),
        out_specs=(P("tm", "freq", None), P(), P()),
        check_vma=False,
    )
```

```python
import functools

import jax
import jax.numpy as jnp
from jax import lax
from jax.experimental import pallas as pl
from jax.experimental.pallas import tpu as pltpu
from jax.sharding import PartitionSpec as P

HEADS = 4
HALF = 64
EPS = 1e-06
MASKED = -1e30
BF = jnp.bfloat16
F32 = jnp.float32
MESH = pl.DeviceIdType.MESH
SEMAPHORES = 42
NEAR = 4
VMEM_SPEC = pl.BlockSpec(memory_space=pltpu.VMEM)


def dot(a, b):
    return lax.dot_general(a, b, (((1,), (0,)), ((), ())), preferred_element_type=F32)


def dot_t(a, b):
    return lax.dot_general(a, b, (((1,), (1,)), ((), ())), preferred_element_type=F32)


def t_dot(a, b):
    return lax.dot_general(a, b, (((0,), (0,)), ((), ())), preferred_element_type=F32)


def unit(rows):
    inverse = lax.rsqrt(jnp.mean(rows * rows, axis=-1, keepdims=True) + EPS)
    return inverse, rows * inverse


def unit_backward(incoming, inverse, unit_rows, gain):
    scaled = incoming * gain
    mean = jnp.mean(scaled * unit_rows, axis=-1, keepdims=True)
    return inverse * (scaled - unit_rows * mean)


class Exchange:
    def __init__(self, count, me, device_of, source_of, target_of, arrivals, sems):
        self.count, self.me, self.device_of = count, me, device_of
        self.source_of, self.target_of, self.arrivals, self.sems = source_of, target_of, arrivals, sems

    def start(self):
        send_sem, recv_sem = self.sems

        def step(k, carry):
            p = lax.rem(self.me + k, self.count)
            pltpu.make_async_remote_copy(
                src_ref=self.source_of(p),
                dst_ref=self.target_of(self.me),
                send_sem=send_sem,
                recv_sem=recv_sem,
                device_id=self.device_of(p),
                device_id_type=MESH,
            ).start()
            return carry

        lax.fori_loop(1, self.count, step, 0)
        self.target_of(self.me)[...] = self.source_of(self.me)[...]

    def start_range(self, first, count):
        send_sem, recv_sem = self.sems

        def step(k, carry):
            p = first + lax.rem(self.me + k, count)

            @pl.when(p != self.me)
            def _():
                pltpu.make_async_remote_copy(
                    src_ref=self.source_of(p),
                    dst_ref=self.target_of(self.me),
                    send_sem=send_sem,
                    recv_sem=recv_sem,
                    device_id=self.device_of(p),
                    device_id_type=MESH,
                ).start()

            return carry

        lax.fori_loop(0, count, step, 0)

    def keep(self):
        self.target_of(self.me)[...] = self.source_of(self.me)[...]

    def wait(self):
        send_sem, recv_sem = self.sems
        copy = pltpu.make_async_remote_copy(
            src_ref=self.arrivals,
            dst_ref=self.arrivals,
            send_sem=send_sem,
            recv_sem=recv_sem,
            device_id=self.device_of(lax.rem(self.me + 1, self.count)),
            device_id_type=MESH,
        )
        copy.wait_recv()
        copy.wait_send()


class ToTime:
    def __init__(self, bins, me, source, target, sems):
        self.bins, self.halo, self.me = bins, bins // 2, me
        self.mine = lax.div(me, bins)
        self.source, self.target, self.sems = source, target, sems

    def copy(self, source, target, half, device):
        return pltpu.make_async_remote_copy(
            src_ref=source,
            dst_ref=target,
            send_sem=self.sems[half],
            recv_sem=self.sems[2],
            device_id={"tm": device},
            device_id_type=MESH,
        )

    def each_half(self, action):
        for half in range(2):
            needed = (self.me < self.bins + self.halo) if half == 0 else (self.me >= self.halo)
            pl.when(needed)(functools.partial(action, half))

    def start(self):
        def send(half):
            def step(k, carry):
                bin_id = lax.rem(self.me + k, self.bins)
                device = bin_id + self.bins * half

                @pl.when(device != self.me)
                def _():
                    slot = self.target.at[self.me - self.halo * half]
                    self.copy(self.source.at[bin_id], slot, half, device).start()

                return carry

            lax.fori_loop(0, self.bins, step, 0)

        self.each_half(send)
        own = self.me - self.halo * self.mine
        self.target[own] = self.source[self.me - self.bins * self.mine]

    def wait(self):
        other = lax.rem(self.me + 1, 2 * self.bins)
        arrivals = self.target.at[pl.ds(0, self.bins + self.halo - 1)]
        self.copy(arrivals, arrivals, 0, other).wait_recv()

        def sent(half):
            @pl.when(self.mine == half)
            def _():
                left = self.source.at[pl.ds(0, self.bins - 1)]
                self.copy(left, left, half, other).wait_send()

            @pl.when(self.mine != half)
            def _():
                self.copy(self.source, self.source, half, other).wait_send()

        self.each_half(sent)


def total(ref, count):
    return lax.fori_loop(1, count, lambda i, acc: acc + ref[i].astype(F32), ref[0].astype(F32))


def swapped(value):
    return jnp.swapaxes(value.astype(F32), 0, 1).astype(BF)


def head_masks(rows, width):
    lane = lax.broadcasted_iota(jnp.int32, (rows, width), 1) // (width // HEADS)
    return [(lane == head).astype(BF) for head in range(HEADS)]


def weights_of(scores):
    e = jnp.exp(scores - jnp.max(scores, axis=0, keepdims=True))
    return e * (1.0 / jnp.sum(e, axis=0, keepdims=True))


def scores_backward(p, dp):
    return (p * (dp - jnp.sum(dp * p, axis=0, keepdims=True))).astype(BF)


def layer_kernel(
    scale_out, names, x_hbm, up_hbm, gain_hbm, w_hbm, gi_ref, sum_ref, gain_out,
    x_ref, up_ref, gain_ref, w_ref, dma, load_sem, *scratch
):
    s = dict(zip(names, scratch))
    frames, bins, width = x_ref.shape
    scale = (width // HEADS) ** (-0.5)
    tm, freq = lax.axis_index("tm"), lax.axis_index("freq")
    plane, columns = s["wg_time"].shape[0], s["rs_time"].shape[0]
    tm_count, freq_count = columns * NEAR, frames
    core, high = lax.rem(freq, 2), lax.div(freq, 2)
    low, column = lax.rem(tm, NEAR), lax.div(tm, NEAR)
    mine, theirs = core * columns, (1 - core) * columns
    far = freq_count // 2
    rows = bins * freq_count
    base = lax.div(tm, bins) * bins

    def in_freq(p):
        return {"freq": p}

    def in_tm(p):
        return {"tm": p}

    def in_half(p):
        return {"tm": base + p}

    def in_columns(p):
        return {"tm": p * NEAR + low}

    def in_near(p):
        return {"tm": column * NEAR + p, "freq": freq}

    def in_far(p):
        return {"tm": tm, "freq": p * 2 + core}

    used = [0]

    def sems(count=2):
        first = used[0]
        used[0] += count
        return [dma.at[first + i] for i in range(count)]

    def along(group, source_of, target):
        count, me, device_of = group
        arrivals = target.at[pl.ds(0, count - 1)]
        return Exchange(count, me, device_of, source_of, lambda p: target.at[p], arrivals, sems())

    freq_group = (freq_count, freq, in_freq)
    column_group = (columns, column, in_columns)
    near_group = (NEAR, low, in_near)
    far_group = (far, high, in_far)

    pairs = ((x_hbm, x_ref), (up_hbm, up_ref), (gain_hbm, gain_ref), (w_hbm, w_ref))
    loads = [pltpu.make_async_copy(a, b, load_sem.at[i]) for i, (a, b) in enumerate(pairs)]
    for load in loads:
        load.start()

    barrier = pltpu.get_barrier_semaphore()

    def tell(first, last, peer_of):
        def step(k, carry):
            pl.semaphore_signal(barrier, inc=1, device_id=peer_of(k), device_id_type=MESH)
            return carry

        lax.fori_loop(first, last, step, 0)

    tell(1, freq_count, lambda k: in_freq(lax.rem(freq + k, freq_count)))
    tell(1, tm_count, lambda k: in_tm(lax.rem(tm + k, tm_count)))
    for load in loads[:3]:
        load.wait()
    s["up_t"][...] = swapped(up_ref[...])
    pl.semaphore_wait(barrier, freq_count - 1 + tm_count - 1)

    to_frames = along(freq_group, lambda p: x_ref.at[p], s["x_f"])
    to_frames.start()
    up_time = ToTime(bins, tm, s["up_t"], s["up_w"], sems(3))
    up_time.start()
    loads[3].wait()
    to_frames.wait()

    masks = head_masks(rows, width)
    gain = gain_ref[0:1, :]
    x = s["x_f"][...].astype(F32).reshape(rows, width)
    _, unit_rows = unit(x)
    norm = (unit_rows * gain).astype(BF)
    s["n1"][...] = norm
    s["q1"][...] = (dot(norm, w_ref[0]).astype(BF) * scale).astype(BF)
    s["k1"][...] = dot(norm, w_ref[1]).astype(BF)
    s["v1"][...] = dot(norm, w_ref[2]).astype(BF)
    mixed = jnp.zeros((rows, width), F32)
    for head in range(HEADS):
        p = weights_of(dot_t(s["k1"][...], s["q1"][...] * masks[head]))
        s["p1"][head] = p
        mixed = mixed + t_dot(p.astype(BF), s["v1"][...] * masks[head])
    s["o1"][...] = mixed.astype(BF)
    hidden = x + dot(s["o1"][...], w_ref[3])
    s["h_f"][...] = hidden.reshape(x_ref.shape).astype(BF)
    h_back = along(freq_group, lambda p: s["h_f"].at[p], s["h_l"])
    h_back.start()

    up_time.wait()
    blocks, sub = s["up_w"].shape[:2]
    all_rows, own = blocks * sub, bins * sub
    s["up"][...] = s["up_w"][...].astype(F32).reshape(all_rows, width).astype(BF)
    s["go2"][...] = dot_t(s["up"][...], w_ref[7]).astype(BF)
    s["gk2"][...] = jnp.zeros_like(s["gk2"])
    s["gv2"][...] = jnp.zeros_like(s["gv2"])
    h_back.wait()
    s["h_t"][...] = swapped(s["h_l"][...])
    h_time = ToTime(bins, tm, s["h_t"], s["h_w"], sems(3))
    h_time.start()
    h_time.wait()

    gain = gain_ref[1:2, :]
    _, unit_rows = unit(s["h_w"][...].astype(F32).reshape(all_rows, width))
    norm = (unit_rows * gain).astype(BF)
    s["n2"][...] = norm
    s["q2"][...] = (dot(norm, w_ref[4]).astype(BF) * scale).astype(BF)
    s["k2"][...] = dot(norm, w_ref[5]).astype(BF)
    s["v2"][...] = dot(norm, w_ref[6]).astype(BF)
    queries, keys = 2 * HALF, 4 * HALF
    offset = lax.broadcasted_iota(jnp.int32, (keys, queries), 0) - lax.broadcasted_iota(
        jnp.int32, (keys, queries), 1
    )

    half = lax.div(tm, bins)

    def block(n, carry):
        i = n + half * (all_rows // queries - 1 - 2 * n)
        q_at = pl.ds(pl.multiple_of(i * queries, queries), queries)
        k_at = pl.ds(pl.multiple_of(i * HALF, HALF), keys)
        q, go, k, v = s["q2"][q_at, :], s["go2"][q_at, :], s["k2"][k_at, :], s["v2"][k_at, :]
        distance = offset - HALF * i
        allowed = (distance >= -HALF) & (distance < HALF)
        key_masks, query_masks = head_masks(keys, width), head_masks(queries, width)
        mixed = jnp.zeros((queries, width), F32)
        gq = jnp.zeros((queries, width), F32)
        gk = jnp.zeros((keys, width), F32)
        gv = jnp.zeros((keys, width), F32)
        for head in range(HEADS):
            q_head, go_head = q * query_masks[head], go * query_masks[head]
            p = weights_of(jnp.where(allowed, dot_t(k, q_head), MASKED))
            p_half = p.astype(BF)
            ds = scores_backward(p, dot_t(v, go_head))
            mixed = mixed + t_dot(p_half, v * key_masks[head])
            gq = gq + t_dot(ds, k * key_masks[head])
            gk = gk + dot(ds, q_head)
            gv = gv + dot(p_half, go_head)
        s["o2"][q_at, :] = mixed.astype(BF)
        s["gq2"][q_at, :] = (gq * scale).astype(BF)
        s["gk2"][k_at, :] += gk
        s["gv2"][k_at, :] += gv
        return carry

    gh_back = along((bins, tm - base, in_half), lambda p: s["gh_t"].at[p], s["gh_b"])
    first = half * (bins // 2)

    def finish(part):
        many = own // 2
        some = many // sub
        skip = (part + half * (1 - 2 * part)) * some
        mine_at = pl.ds(skip, some)
        at = pl.ds(pl.multiple_of((first + skip) * sub, many), many)
        gq, gk, gv = s["gq2"][at, :], s["gk2"][at, :].astype(BF), s["gv2"][at, :].astype(BF)
        gn = dot_t(gq, w_ref[4]) + dot_t(gk, w_ref[5]) + dot_t(gv, w_ref[6])
        inverse, unit_own = unit(s["h_w"][pl.ds(first + skip, some)].astype(F32).reshape(many, width))
        gh = s["up"][at, :].astype(F32) + unit_backward(gn, inverse, unit_own, gain)
        s["gh_t"][mine_at] = gh.reshape(some, sub, width).astype(BF)
        sums = jnp.sum(gn * unit_own, axis=0, keepdims=True) * scale_out
        s["time_gain"][...] = sums if part == 0 else s["time_gain"][...] + sums
        gh_back.start_range(skip, some)

    lax.fori_loop(0, all_rows // queries - 1, block, 0)
    finish(0)
    block(all_rows // queries - 1, 0)
    finish(1)
    gh_back.keep()
    at = pl.ds(pl.multiple_of(first * sub, own // 2), own)
    upstream = s["up"][at, :]
    gq, gk, gv = s["gq2"][at, :], s["gk2"][at, :].astype(BF), s["gv2"][at, :].astype(BF)

    def place(name, index, value):
        part = (value * scale_out).reshape((plane, width // plane, width)).astype(BF)
        s["wg_" + name][:, index] = part

    def to_partner(source, target):
        send_sem, recv_sem = sems()
        return pltpu.make_async_remote_copy(
            src_ref=source,
            dst_ref=target,
            send_sem=send_sem,
            recv_sem=recv_sem,
            device_id={"freq": freq + 1 - 2 * core},
            device_id_type=MESH,
        )

    def halve(name, index, count):
        at = pl.ds(index, count)
        return to_partner(s["wg_" + name].at[pl.ds(theirs, columns), at], s["pair_" + name].at[:, at])

    def add_pair(name, index, count):
        at = pl.ds(index, count)
        own = s["wg_" + name][pl.ds(mine, columns), at].astype(F32)
        s["both_" + name][:, at] = (own + s["pair_" + name][:, at].astype(F32)).astype(BF)

    def broadcast(group, name, source):
        return along(group, lambda p: s[source], s[name])

    def later_stages(name, result):
        part = result.at[pl.ds(mine, columns)]
        return [
            along(column_group, lambda p: s["both_" + name].at[p], s["rs_" + name]),
            broadcast(near_group, "near_" + name, "near_src_" + name),
            broadcast(far_group, "far_" + name, "far_src_" + name),
            along(column_group, lambda p: s["last_src_" + name], part),
            to_partner(part, part),
        ]

    def add_up(source, count, target):
        s[target][...] = total(s[source], count).astype(s[target].dtype)

    norm = s["n2"][at, :]
    place("time", 0, t_dot(norm, gq))
    place("time", 1, t_dot(norm, gk))
    place("time", 2, t_dot(norm, gv))
    place("time", 3, t_dot(s["o2"][at, :], upstream))
    t_pair = halve("time", 0, 4)
    t_plane, t_near, t_far, t_last, t_out = later_stages("time", sum_ref.at[1])
    t_pair.start()
    t_pair.wait()
    add_pair("time", 0, 4)
    t_plane.start()
    gh_back.wait()
    s["gh_l"][...] = swapped(s["gh_b"][...])
    gh_frames = along(freq_group, lambda p: s["gh_l"].at[p], s["gh_f"])
    gh_frames.start()
    t_plane.wait()
    add_up("rs_time", columns, "near_src_time")
    t_near.start()
    t_near.wait()
    add_up("near_time", NEAR, "far_src_time")
    t_far.start()
    gh_frames.wait()

    f_pairs = [halve("freq", 3, 2), halve("freq", 0, 3)]
    f_plane, f_near, f_far, f_last, f_out = later_stages("freq", sum_ref.at[0])
    gh32 = s["gh_f"][...].astype(F32).reshape(rows, width)
    gh = gh32.astype(BF)
    go = dot_t(gh, w_ref[3]).astype(BF)
    place("freq", 4, t_dot(s["o1"][...], gh))
    gv = jnp.zeros((rows, width), F32)
    for head in range(HEADS):
        gv = gv + dot(s["p1"][head].astype(BF), go * masks[head])
    gv = gv.astype(BF)
    place("freq", 3, t_dot(s["n1"][...], gv))
    f_pairs[0].start()
    gq = jnp.zeros((rows, width), F32)
    gk = jnp.zeros((rows, width), F32)
    for head in range(HEADS):
        ds = scores_backward(s["p1"][head], dot_t(s["v1"][...], go * masks[head]))
        gq = gq + t_dot(ds, s["k1"][...] * masks[head])
        gk = gk + dot(ds, s["q1"][...] * masks[head])
    gq, gk = (gq * scale).astype(BF), gk.astype(BF)
    norm = s["n1"][...]
    place("freq", 1, t_dot(norm, gq))
    place("freq", 2, t_dot(norm, gk))
    gain = gain_ref[0:1, :]
    inverse, unit_rows = unit(s["x_f"][...].astype(F32).reshape(rows, width))
    gn = dot_t(gq, w_ref[0]) + dot_t(gk, w_ref[1]) + dot_t(gv, w_ref[2])
    freq_gain = jnp.sum(gn * unit_rows, axis=0, keepdims=True) * scale_out
    gain_rows = jnp.concatenate(
        [freq_gain, s["time_gain"][...], jnp.zeros((width // plane - 2, width), F32)], axis=0
    )
    s["wg_freq"][:, 0] = jnp.broadcast_to(gain_rows[None], (plane,) + gain_rows.shape).astype(BF)
    f_pairs[1].start()
    f_pairs[0].wait()
    add_pair("freq", 3, 2)
    gi = gh32 + unit_backward(gn, inverse, unit_rows, gain)
    s["gi_f"][...] = gi.reshape(x_ref.shape).astype(BF)
    f_pairs[1].wait()
    add_pair("freq", 0, 3)
    f_plane.start()
    gi_back = along(freq_group, lambda p: s["gi_f"].at[p], gi_ref)
    gi_back.start()

    f_plane.wait()
    add_up("rs_freq", columns, "near_src_freq")
    f_near.start()
    t_far.wait()
    add_up("far_time", far, "last_src_time")
    t_last.start()
    f_near.wait()
    add_up("near_freq", NEAR, "far_src_freq")
    f_far.start()
    t_last.wait()
    t_out.start()
    f_far.wait()
    sums = total(s["far_freq"], far)
    s["last_src_freq"][...] = sums[1:].astype(BF)
    f_last.start()
    gain_out[...] = sums[0, 0:2]
    gi_back.wait()
    f_last.wait()
    f_out.start()
    t_out.wait()
    f_out.wait()
    assert used[0] <= SEMAPHORES, used


def finish_kernel(gi_ref, sum_ref, gain_ref, gi_out, w_out, gain_out):
    plane, count, part, width = sum_ref.shape[1:]
    for index in range(count):
        w_out[index] = sum_ref[0, :, index].astype(F32).reshape(plane * part, width)

    @pl.when(pl.program_id(0) == 0)
    def _():
        gi_out[...] = gi_ref[...]
        gain_out[...] = gain_ref[...]


def per_device(features, upstream, weights, gains):
    frames, bins, width = features.shape
    freq_count, tm_count = lax.axis_size("freq"), lax.axis_size("tm")
    rows = bins * freq_count
    scale_out = (frames * tm_count * rows) ** (-0.5)
    shape = jax.ShapeDtypeStruct
    plane, far = tm_count // NEAR * 2, freq_count // 2
    part = width // plane
    span = bins + bins // 2
    all_rows = span * frames

    local = ((frames, bins, width), BF)
    turned = ((bins, frames, width), BF)
    window = ((span, frames, width), BF)
    flat = ((rows, width), BF)
    tall = ((all_rows, width), BF)
    piece = (4, part, width)
    gain = (2, width)
    buffers = dict(
        up_t=turned, up_w=window, x_f=local, n1=flat, q1=flat, k1=flat, v1=flat, o1=flat,
        p1=((HEADS, rows, rows), F32), h_f=local, h_l=local, h_t=turned, h_w=window,
        up=tall, go2=tall, n2=tall, q2=tall, k2=tall, v2=tall, o2=tall, gq2=tall,
        gk2=((all_rows, width), F32), gv2=((all_rows, width), F32),
        gh_t=turned, gh_b=turned, gh_l=local, gh_f=local, gi_f=local,
        time_gain=((1, width), F32),
    )
    for name, pieces in (("freq", 5), ("time", 4)):
        stack = (pieces, part, width)
        buffers["wg_" + name] = ((plane,) + stack, BF)
        for step in ("pair_", "both_", "rs_"):
            buffers[step + name] = ((plane // 2,) + stack, BF)
        buffers["near_src_" + name] = (stack, BF)
        buffers["near_" + name] = ((NEAR,) + stack, BF)
        buffers["far_src_" + name] = (stack, BF)
        buffers["far_" + name] = ((far,) + stack, BF)
        buffers["last_src_" + name] = (piece, BF)
    names = list(buffers)

    outs = pl.pallas_call(
        functools.partial(layer_kernel, scale_out, names),
        out_shape=[
            shape(features.shape, BF),
            shape((2, plane) + piece, BF),
            shape(gain, F32),
        ],
        in_specs=[pl.BlockSpec(memory_space=pl.ANY)] * 4,
        out_specs=[VMEM_SPEC] * 3,
        scratch_shapes=[
            pltpu.VMEM(features.shape, BF),
            pltpu.VMEM(upstream.shape, BF),
            pltpu.VMEM(gain, F32),
            pltpu.VMEM(weights.shape, BF),
            pltpu.SemaphoreType.DMA((SEMAPHORES,)),
            pltpu.SemaphoreType.DMA((4,)),
        ]
        + [pltpu.VMEM(*buffers[name]) for name in names],
        compiler_params=pltpu.CompilerParams(collective_id=0, has_side_effects=True),
        name="layer",
    )(features, upstream, gains, weights)
    whole = [pl.BlockSpec(features.shape, lambda i: (0, 0, 0)), pl.BlockSpec(gain, lambda i: (0, 0))]
    return pl.pallas_call(
        finish_kernel,
        grid=(2,),
        out_shape=[shape(features.shape, BF), shape(weights.shape, F32), shape(gain, F32)],
        in_specs=[
            whole[0],
            pl.BlockSpec((1, plane) + piece, lambda i: (i, 0, 0, 0, 0)),
            whole[1],
        ],
        out_specs=[whole[0], pl.BlockSpec((4, width, width), lambda i: (i, 0, 0)), whole[1]],
        name="finish",
    )(*outs)


def solution(mesh):
    return jax.shard_map(
        per_device,
        mesh=mesh,
        in_specs=(P("tm", "freq", None), P("tm", "freq", None), P(), P()),
        out_specs=(P("tm", "freq", None), P(), P()),
        check_vma=False,
    )
```

```python
import functools

import jax
import jax.numpy as jnp
from jax import lax
from jax.experimental import pallas as pl
from jax.experimental.pallas import tpu as pltpu
from jax.sharding import PartitionSpec as P

HEADS = 4
HALF = 64
EPS = 1e-06
MASKED = -1e30
BF = jnp.bfloat16
F32 = jnp.float32
MESH = pl.DeviceIdType.MESH
SEMAPHORES = 42
NEAR = 4
VMEM_SPEC = pl.BlockSpec(memory_space=pltpu.VMEM)


def dot(a, b):
    return lax.dot_general(a, b, (((1,), (0,)), ((), ())), preferred_element_type=F32)


def dot_t(a, b):
    return lax.dot_general(a, b, (((1,), (1,)), ((), ())), preferred_element_type=F32)


def t_dot(a, b):
    return lax.dot_general(a, b, (((0,), (0,)), ((), ())), preferred_element_type=F32)


def unit(rows):
    inverse = lax.rsqrt(jnp.mean(rows * rows, axis=-1, keepdims=True) + EPS)
    return inverse, rows * inverse


def unit_backward(incoming, inverse, unit_rows, gain):
    scaled = incoming * gain
    mean = jnp.mean(scaled * unit_rows, axis=-1, keepdims=True)
    return inverse * (scaled - unit_rows * mean)


class Exchange:
    def __init__(self, count, me, device_of, source_of, target_of, arrivals, sems):
        self.count, self.me, self.device_of = count, me, device_of
        self.source_of, self.target_of, self.arrivals, self.sems = source_of, target_of, arrivals, sems

    def start(self):
        send_sem, recv_sem = self.sems

        def step(k, carry):
            p = lax.rem(self.me + k, self.count)
            pltpu.make_async_remote_copy(
                src_ref=self.source_of(p),
                dst_ref=self.target_of(self.me),
                send_sem=send_sem,
                recv_sem=recv_sem,
                device_id=self.device_of(p),
                device_id_type=MESH,
            ).start()
            return carry

        lax.fori_loop(1, self.count, step, 0)
        self.target_of(self.me)[...] = self.source_of(self.me)[...]

    def wait(self):
        send_sem, recv_sem = self.sems
        copy = pltpu.make_async_remote_copy(
            src_ref=self.arrivals,
            dst_ref=self.arrivals,
            send_sem=send_sem,
            recv_sem=recv_sem,
            device_id=self.device_of(lax.rem(self.me + 1, self.count)),
            device_id_type=MESH,
        )
        copy.wait_recv()
        copy.wait_send()


class ToTime:
    def __init__(self, bins, me, source, target, sems):
        self.bins, self.halo, self.me = bins, bins // 2, me
        self.mine = lax.div(me, bins)
        self.source, self.target, self.sems = source, target, sems

    def copy(self, source, target, half, device):
        return pltpu.make_async_remote_copy(
            src_ref=source,
            dst_ref=target,
            send_sem=self.sems[half],
            recv_sem=self.sems[2],
            device_id={"tm": device},
            device_id_type=MESH,
        )

    def each_half(self, action):
        for half in range(2):
            needed = (self.me < self.bins + self.halo) if half == 0 else (self.me >= self.halo)
            pl.when(needed)(functools.partial(action, half))

    def start(self):
        def send(half):
            def step(k, carry):
                bin_id = lax.rem(self.me + k, self.bins)
                device = bin_id + self.bins * half

                @pl.when(device != self.me)
                def _():
                    slot = self.target.at[self.me - self.halo * half]
                    self.copy(self.source.at[bin_id], slot, half, device).start()

                return carry

            lax.fori_loop(0, self.bins, step, 0)

        self.each_half(send)
        own = self.me - self.halo * self.mine
        self.target[own] = self.source[self.me - self.bins * self.mine]

    def wait(self):
        other = lax.rem(self.me + 1, 2 * self.bins)
        arrivals = self.target.at[pl.ds(0, self.bins + self.halo - 1)]
        self.copy(arrivals, arrivals, 0, other).wait_recv()

        def sent(half):
            @pl.when(self.mine == half)
            def _():
                left = self.source.at[pl.ds(0, self.bins - 1)]
                self.copy(left, left, half, other).wait_send()

            @pl.when(self.mine != half)
            def _():
                self.copy(self.source, self.source, half, other).wait_send()

        self.each_half(sent)


def total(ref, count):
    return lax.fori_loop(1, count, lambda i, acc: acc + ref[i].astype(F32), ref[0].astype(F32))


def swapped(value):
    return jnp.swapaxes(value.astype(F32), 0, 1).astype(BF)


def head_masks(rows, width):
    lane = lax.broadcasted_iota(jnp.int32, (rows, width), 1) // (width // HEADS)
    return [(lane == head).astype(BF) for head in range(HEADS)]


def weights_of(scores):
    e = jnp.exp(scores - jnp.max(scores, axis=0, keepdims=True))
    return e * (1.0 / jnp.sum(e, axis=0, keepdims=True))


def scores_backward(p, dp):
    return (p * (dp - jnp.sum(dp * p, axis=0, keepdims=True))).astype(BF)


def layer_kernel(
    scale_out, names, x_hbm, up_hbm, gain_hbm, w_hbm, gi_ref, sum_ref, gain_out,
    x_ref, up_ref, gain_ref, w_ref, dma, load_sem, *scratch
):
    s = dict(zip(names, scratch))
    frames, bins, width = x_ref.shape
    scale = (width // HEADS) ** (-0.5)
    tm, freq = lax.axis_index("tm"), lax.axis_index("freq")
    plane, columns = s["wg_time"].shape[0], s["rs_time"].shape[0]
    tm_count, freq_count = columns * NEAR, frames
    core, high = lax.rem(freq, 2), lax.div(freq, 2)
    low, column = lax.rem(tm, NEAR), lax.div(tm, NEAR)
    mine, theirs = core * columns, (1 - core) * columns
    far = freq_count // 2
    rows = bins * freq_count
    base = lax.div(tm, bins) * bins

    def in_freq(p):
        return {"freq": p}

    def in_tm(p):
        return {"tm": p}

    def in_half(p):
        return {"tm": base + p}

    def in_columns(p):
        return {"tm": p * NEAR + low}

    def in_near(p):
        return {"tm": column * NEAR + p, "freq": freq}

    def in_far(p):
        return {"tm": tm, "freq": p * 2 + core}

    used = [0]

    def sems(count=2):
        first = used[0]
        used[0] += count
        return [dma.at[first + i] for i in range(count)]

    def along(group, source_of, target):
        count, me, device_of = group
        arrivals = target.at[pl.ds(0, count - 1)]
        return Exchange(count, me, device_of, source_of, lambda p: target.at[p], arrivals, sems())

    freq_group = (freq_count, freq, in_freq)
    column_group = (columns, column, in_columns)
    near_group = (NEAR, low, in_near)
    far_group = (far, high, in_far)

    pairs = ((x_hbm, x_ref), (up_hbm, up_ref), (gain_hbm, gain_ref), (w_hbm, w_ref))
    loads = [pltpu.make_async_copy(a, b, load_sem.at[i]) for i, (a, b) in enumerate(pairs)]
    for load in loads:
        load.start()

    barrier = pltpu.get_barrier_semaphore()

    def tell(first, last, peer_of):
        def step(k, carry):
            pl.semaphore_signal(barrier, inc=1, device_id=peer_of(k), device_id_type=MESH)
            return carry

        lax.fori_loop(first, last, step, 0)

    tell(1, freq_count, lambda k: in_freq(lax.rem(freq + k, freq_count)))
    tell(1, tm_count, lambda k: in_tm(lax.rem(tm + k, tm_count)))
    for load in loads[:3]:
        load.wait()
    s["up_t"][...] = swapped(up_ref[...])
    pl.semaphore_wait(barrier, freq_count - 1 + tm_count - 1)

    to_frames = along(freq_group, lambda p: x_ref.at[p], s["x_f"])
    to_frames.start()
    up_time = ToTime(bins, tm, s["up_t"], s["up_w"], sems(3))
    up_time.start()
    loads[3].wait()
    to_frames.wait()

    masks = head_masks(rows, width)
    gain = gain_ref[0:1, :]
    x = s["x_f"][...].astype(F32).reshape(rows, width)
    _, unit_rows = unit(x)
    norm = (unit_rows * gain).astype(BF)
    s["n1"][...] = norm
    s["q1"][...] = (dot(norm, w_ref[0]).astype(BF) * scale).astype(BF)
    s["k1"][...] = dot(norm, w_ref[1]).astype(BF)
    s["v1"][...] = dot(norm, w_ref[2]).astype(BF)
    mixed = jnp.zeros((rows, width), F32)
    for head in range(HEADS):
        p = weights_of(dot_t(s["k1"][...], s["q1"][...] * masks[head]))
        s["p1"][head] = p
        mixed = mixed + t_dot(p.astype(BF), s["v1"][...] * masks[head])
    s["o1"][...] = mixed.astype(BF)
    hidden = x + dot(s["o1"][...], w_ref[3])
    s["h_f"][...] = hidden.reshape(x_ref.shape).astype(BF)
    h_back = along(freq_group, lambda p: s["h_f"].at[p], s["h_l"])
    h_back.start()

    up_time.wait()
    blocks, sub = s["up_w"].shape[:2]
    all_rows, own = blocks * sub, bins * sub
    s["up"][...] = s["up_w"][...].astype(F32).reshape(all_rows, width).astype(BF)
    s["go2"][...] = dot_t(s["up"][...], w_ref[7]).astype(BF)
    s["gk2"][...] = jnp.zeros_like(s["gk2"])
    s["gv2"][...] = jnp.zeros_like(s["gv2"])
    h_back.wait()
    s["h_t"][...] = swapped(s["h_l"][...])
    h_time = ToTime(bins, tm, s["h_t"], s["h_w"], sems(3))
    h_time.start()
    h_time.wait()

    gain = gain_ref[1:2, :]
    _, unit_rows = unit(s["h_w"][...].astype(F32).reshape(all_rows, width))
    norm = (unit_rows * gain).astype(BF)
    s["n2"][...] = norm
    s["q2"][...] = (dot(norm, w_ref[4]).astype(BF) * scale).astype(BF)
    s["k2"][...] = dot(norm, w_ref[5]).astype(BF)
    s["v2"][...] = dot(norm, w_ref[6]).astype(BF)
    queries, keys = 2 * HALF, 4 * HALF
    offset = lax.broadcasted_iota(jnp.int32, (keys, queries), 0) - lax.broadcasted_iota(
        jnp.int32, (keys, queries), 1
    )

    def block(i, carry):
        q_at = pl.ds(pl.multiple_of(i * queries, queries), queries)
        k_at = pl.ds(pl.multiple_of(i * HALF, HALF), keys)
        q, go, k, v = s["q2"][q_at, :], s["go2"][q_at, :], s["k2"][k_at, :], s["v2"][k_at, :]
        distance = offset - HALF * i
        allowed = (distance >= -HALF) & (distance < HALF)
        key_masks, query_masks = head_masks(keys, width), head_masks(queries, width)
        mixed = jnp.zeros((queries, width), F32)
        gq = jnp.zeros((queries, width), F32)
        gk = jnp.zeros((keys, width), F32)
        gv = jnp.zeros((keys, width), F32)
        for head in range(HEADS):
            q_head, go_head = q * query_masks[head], go * query_masks[head]
            p = weights_of(jnp.where(allowed, dot_t(k, q_head), MASKED))
            p_half = p.astype(BF)
            ds = scores_backward(p, dot_t(v, go_head))
            mixed = mixed + t_dot(p_half, v * key_masks[head])
            gq = gq + t_dot(ds, k * key_masks[head])
            gk = gk + dot(ds, q_head)
            gv = gv + dot(p_half, go_head)
        s["o2"][q_at, :] = mixed.astype(BF)
        s["gq2"][q_at, :] = (gq * scale).astype(BF)
        s["gk2"][k_at, :] += gk
        s["gv2"][k_at, :] += gv
        return carry

    lax.fori_loop(0, all_rows // queries, block, 0)

    half = lax.div(tm, bins)
    first = pl.multiple_of(half * (own // 2), own // 2)
    at = pl.ds(first, own)
    gq, gk, gv = s["gq2"][at, :], s["gk2"][at, :].astype(BF), s["gv2"][at, :].astype(BF)
    gn = dot_t(gq, w_ref[4]) + dot_t(gk, w_ref[5]) + dot_t(gv, w_ref[6])
    own_blocks = pl.ds(half * (bins // 2), bins)
    inverse, unit_own = unit(s["h_w"][own_blocks].astype(F32).reshape(own, width))
    upstream = s["up"][at, :]
    gh = upstream.astype(F32) + unit_backward(gn, inverse, unit_own, gain)
    s["gh_t"][...] = gh.reshape(bins, sub, width).astype(BF)
    gh_back = along((bins, tm - base, in_half), lambda p: s["gh_t"].at[p], s["gh_b"])
    gh_back.start()

    def place(name, index, value):
        part = (value * scale_out).reshape((plane, width // plane, width)).astype(BF)
        s["wg_" + name][:, index] = part

    def to_partner(source, target):
        send_sem, recv_sem = sems()
        return pltpu.make_async_remote_copy(
            src_ref=source,
            dst_ref=target,
            send_sem=send_sem,
            recv_sem=recv_sem,
            device_id={"freq": freq + 1 - 2 * core},
            device_id_type=MESH,
        )

    def halve(name, index, count):
        at = pl.ds(index, count)
        return to_partner(s["wg_" + name].at[pl.ds(theirs, columns), at], s["pair_" + name].at[:, at])

    def add_pair(name, index, count):
        at = pl.ds(index, count)
        own = s["wg_" + name][pl.ds(mine, columns), at].astype(F32)
        s["both_" + name][:, at] = (own + s["pair_" + name][:, at].astype(F32)).astype(BF)

    def broadcast(group, name, source):
        return along(group, lambda p: s[source], s[name])

    def later_stages(name, result):
        part = result.at[pl.ds(mine, columns)]
        return [
            along(column_group, lambda p: s["both_" + name].at[p], s["rs_" + name]),
            broadcast(near_group, "near_" + name, "near_src_" + name),
            broadcast(far_group, "far_" + name, "far_src_" + name),
            along(column_group, lambda p: s["last_src_" + name], part),
            to_partner(part, part),
        ]

    def add_up(source, count, target):
        s[target][...] = total(s[source], count).astype(s[target].dtype)

    norm = s["n2"][at, :]
    place("time", 0, t_dot(norm, gq))
    place("time", 1, t_dot(norm, gk))
    place("time", 2, t_dot(norm, gv))
    place("time", 3, t_dot(s["o2"][at, :], upstream))
    s["time_gain"][...] = jnp.sum(gn * unit_own, axis=0, keepdims=True) * scale_out
    t_pair = halve("time", 0, 4)
    t_plane, t_near, t_far, t_last, t_out = later_stages("time", sum_ref.at[1])
    t_pair.start()
    t_pair.wait()
    add_pair("time", 0, 4)
    t_plane.start()
    gh_back.wait()
    s["gh_l"][...] = swapped(s["gh_b"][...])
    gh_frames = along(freq_group, lambda p: s["gh_l"].at[p], s["gh_f"])
    gh_frames.start()
    t_plane.wait()
    add_up("rs_time", columns, "near_src_time")
    t_near.start()
    t_near.wait()
    add_up("near_time", NEAR, "far_src_time")
    t_far.start()
    gh_frames.wait()

    f_pairs = [halve("freq", 3, 2), halve("freq", 0, 3)]
    f_plane, f_near, f_far, f_last, f_out = later_stages("freq", sum_ref.at[0])
    gh32 = s["gh_f"][...].astype(F32).reshape(rows, width)
    gh = gh32.astype(BF)
    go = dot_t(gh, w_ref[3]).astype(BF)
    place("freq", 4, t_dot(s["o1"][...], gh))
    gv = jnp.zeros((rows, width), F32)
    for head in range(HEADS):
        gv = gv + dot(s["p1"][head].astype(BF), go * masks[head])
    gv = gv.astype(BF)
    place("freq", 3, t_dot(s["n1"][...], gv))
    f_pairs[0].start()
    gq = jnp.zeros((rows, width), F32)
    gk = jnp.zeros((rows, width), F32)
    for head in range(HEADS):
        ds = scores_backward(s["p1"][head], dot_t(s["v1"][...], go * masks[head]))
        gq = gq + t_dot(ds, s["k1"][...] * masks[head])
        gk = gk + dot(ds, s["q1"][...] * masks[head])
    gq, gk = (gq * scale).astype(BF), gk.astype(BF)
    norm = s["n1"][...]
    place("freq", 1, t_dot(norm, gq))
    place("freq", 2, t_dot(norm, gk))
    gain = gain_ref[0:1, :]
    inverse, unit_rows = unit(s["x_f"][...].astype(F32).reshape(rows, width))
    gn = dot_t(gq, w_ref[0]) + dot_t(gk, w_ref[1]) + dot_t(gv, w_ref[2])
    freq_gain = jnp.sum(gn * unit_rows, axis=0, keepdims=True) * scale_out
    gain_rows = jnp.concatenate(
        [freq_gain, s["time_gain"][...], jnp.zeros((width // plane - 2, width), F32)], axis=0
    )
    s["wg_freq"][:, 0] = jnp.broadcast_to(gain_rows[None], (plane,) + gain_rows.shape).astype(BF)
    f_pairs[1].start()
    f_pairs[0].wait()
    add_pair("freq", 3, 2)
    gi = gh32 + unit_backward(gn, inverse, unit_rows, gain)
    s["gi_f"][...] = gi.reshape(x_ref.shape).astype(BF)
    f_pairs[1].wait()
    add_pair("freq", 0, 3)
    f_plane.start()
    gi_back = along(freq_group, lambda p: s["gi_f"].at[p], gi_ref)
    gi_back.start()

    f_plane.wait()
    add_up("rs_freq", columns, "near_src_freq")
    f_near.start()
    t_far.wait()
    add_up("far_time", far, "last_src_time")
    t_last.start()
    f_near.wait()
    add_up("near_freq", NEAR, "far_src_freq")
    f_far.start()
    t_last.wait()
    t_out.start()
    f_far.wait()
    sums = total(s["far_freq"], far)
    s["last_src_freq"][...] = sums[1:].astype(BF)
    f_last.start()
    gain_out[...] = sums[0, 0:2]
    gi_back.wait()
    f_last.wait()
    f_out.start()
    t_out.wait()
    f_out.wait()
    assert used[0] <= SEMAPHORES, used


def finish_kernel(gi_hbm, sum_hbm, gain_hbm, gi_out, w_out, gain_out, gi, sums, gain, whole, come, leave):
    sets, plane, count, part, width = sums.shape
    loads = [pltpu.make_async_copy(sum_hbm.at[i], sums.at[i], come.at[i]) for i in range(sets)]
    small = [
        pltpu.make_async_copy(gi_hbm, gi, come.at[sets]),
        pltpu.make_async_copy(gain_hbm, gain, come.at[sets + 1]),
    ]
    stores = [
        pltpu.make_async_copy(gi, gi_out, leave.at[0]),
        pltpu.make_async_copy(gain, gain_out, leave.at[1]),
    ]
    for copy in loads + small:
        copy.start()
    for i in range(sets):
        loads[i].wait()
        for j in range(count):
            m = i * count + j
            whole[m] = sums[i, :, j].astype(F32).reshape(plane * part, width)
            stores.append(pltpu.make_async_copy(whole.at[m], w_out.at[m], leave.at[2 + m]))
            stores[-1].start()
        if i == 0:
            for load, store in zip(small, stores[:2]):
                load.wait()
                store.start()
    for store in stores:
        store.wait()


def per_device(features, upstream, weights, gains):
    frames, bins, width = features.shape
    freq_count, tm_count = lax.axis_size("freq"), lax.axis_size("tm")
    rows = bins * freq_count
    scale_out = (frames * tm_count * rows) ** (-0.5)
    shape = jax.ShapeDtypeStruct
    plane, far = tm_count // NEAR * 2, freq_count // 2
    part = width // plane
    span = bins + bins // 2
    all_rows = span * frames

    local = ((frames, bins, width), BF)
    turned = ((bins, frames, width), BF)
    window = ((span, frames, width), BF)
    flat = ((rows, width), BF)
    tall = ((all_rows, width), BF)
    piece = (4, part, width)
    gain = (2, width)
    buffers = dict(
        up_t=turned, up_w=window, x_f=local, n1=flat, q1=flat, k1=flat, v1=flat, o1=flat,
        p1=((HEADS, rows, rows), F32), h_f=local, h_l=local, h_t=turned, h_w=window,
        up=tall, go2=tall, n2=tall, q2=tall, k2=tall, v2=tall, o2=tall, gq2=tall,
        gk2=((all_rows, width), F32), gv2=((all_rows, width), F32),
        gh_t=turned, gh_b=turned, gh_l=local, gh_f=local, gi_f=local,
        time_gain=((1, width), F32),
    )
    for name, pieces in (("freq", 5), ("time", 4)):
        stack = (pieces, part, width)
        buffers["wg_" + name] = ((plane,) + stack, BF)
        for step in ("pair_", "both_", "rs_"):
            buffers[step + name] = ((plane // 2,) + stack, BF)
        buffers["near_src_" + name] = (stack, BF)
        buffers["near_" + name] = ((NEAR,) + stack, BF)
        buffers["far_src_" + name] = (stack, BF)
        buffers["far_" + name] = ((far,) + stack, BF)
        buffers["last_src_" + name] = (piece, BF)
    names = list(buffers)

    outs = pl.pallas_call(
        functools.partial(layer_kernel, scale_out, names),
        out_shape=[
            shape(features.shape, BF),
            shape((2, plane) + piece, BF),
            shape(gain, F32),
        ],
        in_specs=[pl.BlockSpec(memory_space=pl.ANY)] * 4,
        out_specs=[VMEM_SPEC] * 3,
        scratch_shapes=[
            pltpu.VMEM(features.shape, BF),
            pltpu.VMEM(upstream.shape, BF),
            pltpu.VMEM(gain, F32),
            pltpu.VMEM(weights.shape, BF),
            pltpu.SemaphoreType.DMA((SEMAPHORES,)),
            pltpu.SemaphoreType.DMA((4,)),
        ]
        + [pltpu.VMEM(*buffers[name]) for name in names],
        compiler_params=pltpu.CompilerParams(collective_id=0, has_side_effects=True),
        name="layer",
    )(features, upstream, gains, weights)
    anywhere = pl.BlockSpec(memory_space=pl.ANY)
    return pl.pallas_call(
        finish_kernel,
        out_shape=[shape(features.shape, BF), shape(weights.shape, F32), shape(gain, F32)],
        in_specs=[anywhere] * 3,
        out_specs=[anywhere] * 3,
        scratch_shapes=[
            pltpu.VMEM(features.shape, BF),
            pltpu.VMEM((2, plane) + piece, BF),
            pltpu.VMEM(gain, F32),
            pltpu.VMEM(weights.shape, F32),
            pltpu.SemaphoreType.DMA((4,)),
            pltpu.SemaphoreType.DMA((10,)),
        ],
        name="finish",
    )(*outs)


def solution(mesh):
    return jax.shard_map(
        per_device,
        mesh=mesh,
        in_specs=(P("tm", "freq", None), P("tm", "freq", None), P(), P()),
        out_specs=(P("tm", "freq", None), P(), P()),
        check_vma=False,
    )
```
